512 devices in a mesh: sector: 16 (over y, z_hi), block: 16 (over z_lo, x), flame: 2 (over core).
Axes of the slice: x: 4, y: 8, z: 8 (z_hi: 2, z_lo: 4; z = z_hi * 4 + z_lo), core: 2. Of those that a mesh axis runs over, the one named last changes fastest.
Arguments:
- rhs_direct: float32 [128, 256, 512], P('sector', 'block', 'flame'), may hold values from -6 to 6
- rhs_adjoint: float32 [128, 256, 512], P('sector', 'block', 'flame'), may hold values from -6 to 6
- diag_shift: float32 [128, 256, 512], P('sector', 'block', 'flame'), may hold values from 1 to 3
- flame_gain: float32 [128, 256, 512], P('sector', 'block', 'flame'), may hold values from -0.6 to 0.6
- ref_owner: int32 [128, 256, 512], P('sector', 'block', 'flame'), may hold values from 0 to 255
Outputs:
- field_first: float32 [128, 256, 512], P('sector', 'block', 'flame')
- field_second: float32 [128, 256, 512], P('sector', 'block', 'flame')
The draws below stay inside these ranges and needn't reach their ends.
All inputs are finite; a program needn't handle non-finite values.
Results may differ from the reference program's by a relative error of at most 0.00018.
Values sent between devices are 32-bit elements; how exact they have to be, the bound alone decides.
No kernel may reach another device: no remote copies, remote signals or barrier semaphores. Data moves between devices by JAX's collectives and lax.ppermute only.
A program may use at most 64 MiB of HBM per device.

```python
import math
import jax
import jax.numpy as jnp
import numpy as np
from jax import lax

CA = 8
CX = 16
CR = 256
REF_DEV = 8
ITERS = 6
REFS = 256
NA = 128
NX = 256
NR = 512


def place_ends(result, own_key, smallest, largest):
    longest = result.shape.index(max(result.shape))
    spots = []
    for shift in (0, 1):
        where = [jax.random.randint(jax.random.fold_in(own_key, axis), (), 0, length) for axis, length in enumerate(result.shape)]
        where[longest] = (where[longest] + shift) % result.shape[longest]
        spots.append(tuple(where))
    return result.at[spots[0]].set(smallest).at[spots[1]].set(largest)


def block_levels(rng, dims, cuts, low, largest):
    factor_of = 1.0
    for position, blocks in cuts:
        draws = jax.random.uniform(jax.random.fold_in(jax.random.fold_in(rng, 6), position), (blocks,), jnp.float32, low / len(cuts), largest / len(cuts))
        factor_of = factor_of * jnp.repeat(jnp.exp(draws), dims[position] // blocks).reshape((-1,) + (1,) * (len(dims) - 1 - position))
    return factor_of


def rank_bounds(number_of, skew):
    portions = [(1 << 20) // math.isqrt(rank ** skew) + 1 for rank in range(1, number_of + 1)]
    spread = 1 + sum(portions) // (1 << 30)
    return np.cumsum(np.array([max(1, weight // spread) for weight in portions]))


def ranked(rng, dims, number_of, slope):
    listing = rank_bounds(number_of, slope)
    lot = jax.random.randint(jax.random.fold_in(rng, 1), dims, 0, int(listing[number_of - 1]))
    rank = jnp.searchsorted(jnp.asarray(listing, jnp.int32), lot, side="right")
    return jax.random.permutation(jax.random.fold_in(rng, 2), number_of)[rank].astype(jnp.int32)


def centred(own_key, dims, deviation, limit, pieces=(), kind=jnp.bfloat16):
    array = jax.random.normal(own_key, dims, jnp.float32) * deviation
    if len(pieces) > 0:
        array = block_levels(own_key, dims, pieces, -0.22, 0.18) * array
    return jnp.clip(array, min=-limit, max=limit).astype(kind)


def setup_inputs(seed: int = 0) -> dict:
    key_list = jax.random.split(jax.random.key(seed), 6)
    return {
        "rhs_direct": centred(key_list[0], (NA, NX, NR), 1.0, 6.0, ((0, 16), (1, 16), (2, 2)), jnp.float32),
        "rhs_adjoint": centred(key_list[1], (NA, NX, NR), 1.0, 6.0, ((0, 16), (1, 16), (2, 2)), jnp.float32),
        "diag_shift": jnp.clip(1.0 + 2.0 * jax.random.uniform(key_list[2], (NA, NX, NR), jnp.float32) ** block_levels(key_list[2], (NA, NX, NR), ((0, 16), (1, 16), (2, 2)), -0.2, 0.2), 1.0, 3.0),
        "flame_gain": jnp.clip(jax.random.uniform(key_list[3], (NA, NX, NR), jnp.float32, -0.6, 0.6) * block_levels(key_list[3], (NA, NX, NR), ((0, 16), (1, 16), (2, 2)), -0.4, 0.0), -0.6, 0.6),
        "ref_owner": place_ends(ranked(key_list[4], (NA, NX, NR), REFS, 2), jax.random.fold_in(key_list[4], 3), 0, REFS - 1).astype(jnp.int32),
    }


def neighbours(field):
    total = jnp.roll(field, 1, 0) + jnp.roll(field, -1, 0)
    padded = jnp.pad(field, ((0, 0), (1, 1), (1, 1)))
    total = total + padded[:, 2:, 1:-1] + padded[:, :-2, 1:-1]
    return total + padded[:, 1:-1, 2:] + padded[:, 1:-1, :-2]

def ref_table(field):
    spacing = CR // REF_DEV
    picked = field[::CA, ::CX, ::spacing]
    return picked.reshape(picked.shape[0], -1)

def flame_direct(field, flame_gain, ref_owner):
    table = ref_table(field)
    sector_ids = (jnp.arange(field.shape[0], dtype=jnp.int32) // CA).astype(jnp.int32)
    looked = table[sector_ids[:, None, None], ref_owner]
    return flame_gain * looked

def flame_adjoint(field, flame_gain, ref_owner):
    spacing = CR // REF_DEV
    sectors = field.shape[0] // CA
    ref_count = field.shape[1] // CX * (field.shape[2] // spacing)
    sector_ids = (jnp.arange(field.shape[0], dtype=jnp.int32) // CA).astype(jnp.int32)
    segment = sector_ids[:, None, None] * ref_count + ref_owner
    sums = jax.ops.segment_sum((flame_gain * field).ravel(), segment.ravel().astype(jnp.int32), num_segments=sectors * ref_count)
    placed = sums.reshape(sectors, field.shape[1] // CX, field.shape[2] // spacing)
    return jnp.zeros_like(field).at[::CA, ::CX, ::spacing].set(placed)

def reference(rhs_direct, rhs_adjoint, diag_shift, flame_gain, ref_owner):
    inverse = 1.0 / (6.0 + diag_shift)
    direct = rhs_direct * inverse
    adjoint = rhs_adjoint * inverse
    for sweeps in range(ITERS):
        direct_next = (rhs_direct + neighbours(direct) + flame_direct(direct, flame_gain, ref_owner)) * inverse
        adjoint_next = (rhs_adjoint + neighbours(adjoint) + flame_adjoint(adjoint, flame_gain, ref_owner)) * inverse
        direct, adjoint = (direct_next, adjoint_next)
    scale = lax.rsqrt(jnp.mean(direct * direct) * jnp.mean(adjoint * adjoint) + 1e-12)
    field_first = adjoint * direct * scale
    field_second = adjoint * flame_direct(direct, flame_gain, ref_owner) * scale
    return (field_first, field_second)
```

```python
import functools

import jax
import jax.numpy as jnp
from jax import lax
from jax.experimental import pallas as pl
from jax.experimental.pallas import tpu as pltpu
from jax.sharding import PartitionSpec as P

ITERS = 6
REF_DEV = 8
PAD = 8
LANES = 128
INTERPRET = False
BF = ("block", "flame")


def _call(kernel, out_shape, n_in, scratch=(), name=None):
    vmem = pl.BlockSpec(memory_space=pltpu.VMEM)
    single = not isinstance(out_shape, (tuple, list))
    return pl.pallas_call(
        kernel,
        out_shape=out_shape,
        in_specs=[pl.BlockSpec(memory_space=pltpu.SMEM)] + [vmem] * n_in,
        out_specs=vmem if single else [vmem] * len(out_shape),
        scratch_shapes=list(scratch),
        interpret=INTERPRET,
        name=name,
    )


def _lookup(table, owner):
    low = jnp.take_along_axis(table[0], owner & (LANES - 1), axis=1, mode="promise_in_bounds")
    high = jnp.take_along_axis(table[1], owner & (LANES - 1), axis=1, mode="promise_in_bounds")
    return jnp.where(owner < LANES, low, high)


def _table(total, row):
    return [jnp.broadcast_to(total[row + j : row + j + 1], (8, LANES)) for j in (0, 1)]


def _send_planes(core, refs, inner_ref, outer_ref, planes):
    inner = jnp.where(core == 0, planes - 1, 0)
    for i, ref in enumerate(refs):
        inner_ref[i] = ref[inner]
        outer_ref[i] = ref[planes - 1 - inner]


def init_kernel(scal_ref, ext_ref, inv_ref, own_ref, d_ref, a_ref, inner_ref, outer_ref, *, blocks):
    core, block = scal_ref[0], scal_ref[1]
    _, planes, rows, _ = ext_ref.shape
    for p in range(planes):
        for t in range(rows // 8):
            at = (p, slice(8 * t, 8 * t + 8))
            inv = 1.0 / (6.0 + ext_ref[(2,) + at])
            if t == 0:
                inv = jnp.where(block == 0, 0.0, inv)
            if t == rows // 8 - 1:
                inv = jnp.where(block == blocks - 1, 0.0, inv)
            inv_ref[at] = inv
            own_ref[at] = ext_ref[(4,) + at].astype(jnp.int32)
            d_ref[at] = ext_ref[(0,) + at] * inv
            a_ref[at] = ext_ref[(1,) + at] * inv
    _send_planes(core, (d_ref, a_ref), inner_ref, outer_ref, planes)


def step_kernel(scal_ref, recv_ref, inner_ref, outer_ref, d_ref, a_ref, ext_ref, inv_ref, own_ref,
                dn_ref, an_ref, inner_out, outer_out):
    core, block = scal_ref[0], scal_ref[1]
    planes, rows, width = d_ref.shape
    tiles = rows // 8
    total = jnp.sum(recv_ref[...], axis=0)
    table = _table(total, 0)
    sums = _table(total, 2)
    lane = lax.broadcasted_iota(jnp.int32, (8, LANES), 1)
    sub = lax.broadcasted_iota(jnp.int32, (8, LANES), 0)
    spot = (lane % 32 == 0) & (sub == 0) & (core == 0)
    first = lax.broadcasted_iota(jnp.int32, (8, width), 1) == 0
    last = lax.broadcasted_iota(jnp.int32, (8, width), 1) == width - 1

    def source(blk):
        tab = jnp.where(blk < 8, sums[0], sums[1])
        parts = []
        for j in range(width // LANES):
            at = jnp.bitwise_and(blk, 7) * 16 + 4 * j + lane // 32
            got = jnp.take_along_axis(tab, at & (LANES - 1), axis=1, mode="promise_in_bounds")
            parts.append(jnp.where(spot, got, 0.0))
        return jnp.concatenate(parts, axis=1)

    def near(ref, field, p, t):
        rng = slice(8 * t, 8 * t + 8)
        here = ref[p, rng]
        if p == 0:
            below = jnp.where(core == 0, outer_ref[field, rng], inner_ref[field, rng])
        else:
            below = ref[p - 1, rng]
        if p == planes - 1:
            above = jnp.where(core == 0, inner_ref[field, rng], outer_ref[field, rng])
        else:
            above = ref[p + 1, rng]
        if t == 0:
            back = pltpu.roll(here, 1, 0)
        else:
            back = ref[p, 8 * t - 1 : 8 * t + 7]
        if t == tiles - 1:
            front = pltpu.roll(here, 7, 0)
        else:
            front = ref[p, 8 * t + 1 : 8 * t + 9]
        left = jnp.where(first, 0.0, pltpu.roll(here, 1, 1))
        right = jnp.where(last, 0.0, pltpu.roll(here, width - 1, 1))
        return (below + above) + (back + front) + (left + right)

    for p in range(planes):
        for t in range(tiles):
            at = (p, slice(8 * t, 8 * t + 8))
            inv = inv_ref[at]
            own = own_ref[at]
            looked = jnp.concatenate(
                [_lookup(table, own[:, LANES * j : LANES * (j + 1)]) for j in range(width // LANES)],
                axis=1,
            )
            flame = ext_ref[(3,) + at] * looked
            dn_ref[at] = (ext_ref[(0,) + at] + near(d_ref, 0, p, t) + flame) * inv
            acc = ext_ref[(1,) + at] + near(a_ref, 1, p, t)
            if p == 0 and t == PAD // 8:
                acc = acc + source(block)
            if p == 0 and t == tiles - PAD // 8:
                acc = acc + source(block + 1)
            an_ref[at] = acc * inv
    _send_planes(core, (dn_ref, an_ref), inner_out, outer_out, planes)


def _write_refs(scal_ref, d_ref, out_ref):
    core, block = scal_ref[0], scal_ref[1]
    width = d_ref.shape[2]
    lane = lax.broadcasted_iota(jnp.int32, (8, LANES), 1)
    row = d_ref[0, PAD : PAD + 8]
    got = jnp.zeros((8, LANES), jnp.float32)
    for j in range(width // LANES):
        part = jnp.broadcast_to(row[0:1, LANES * j : LANES * (j + 1)], (8, LANES))
        pick = jnp.take_along_axis(part, (lane & 3) * 32, axis=1, mode="promise_in_bounds")
        got = jnp.where((lane & 15) // 4 == j, pick, got)
    for half in (0, 1):
        mine = (lane // 16 + 8 * half == block) & (core == 0)
        out_ref[:, half] = jnp.broadcast_to(
            jnp.where(mine, got, 0.0)[0:1], (out_ref.shape[0], LANES)
        )


def collect_kernel(scal_ref, d_ref, a_ref, ext_ref, own_ref, out_ref, *split_refs):
    planes, rows, width = d_ref.shape
    tiles = (rows - 2 * PAD) // 8
    _write_refs(scal_ref, d_ref, out_ref)
    for p in range(planes):
        for t in range(tiles):
            at = (p, slice(PAD + 8 * t, PAD + 8 * t + 8))
            y = ext_ref[(3,) + at] * a_ref[at]
            coarse = y.astype(jnp.bfloat16).astype(jnp.float32)
            fine = y - coarse
            upper = own_ref[at] >= LANES
            base = (p * tiles + t) * 64
            terms = (
                jnp.where(upper, 0.0, coarse),
                jnp.where(upper, 0.0, fine),
                jnp.where(upper, coarse, 0.0),
                jnp.where(upper, fine, 0.0),
            )
            for j in range(width // LANES):
                for k, term in enumerate(terms):
                    split_refs[j][pl.ds(base + k, 8, stride=8), :] = term[:, LANES * j : LANES * (j + 1)]
    ids = lax.broadcasted_iota(jnp.int32, (16, width), 0).astype(jnp.float32)
    one = jnp.ones((16, width), jnp.bfloat16)
    zero = jnp.zeros((16, width), jnp.bfloat16)
    groups = [(ids + 16.0 * g).astype(jnp.bfloat16) for g in range(LANES // 16)]
    acc = jnp.zeros((8, LANES), jnp.float32)
    for p in range(planes):
        for t in range(tiles):
            low = (own_ref[p, PAD + 8 * t : PAD + 8 * t + 8] & (LANES - 1)).astype(jnp.float32)
            for x in range(8):
                line = jnp.broadcast_to(low[x : x + 1], (16, width)).astype(jnp.bfloat16)
                hot = jnp.concatenate([jnp.where(line == g, one, zero) for g in groups], axis=0)
                base = ((p * tiles + t) * 8 + x) * 8
                vals = jnp.concatenate(
                    [ref[base : base + 8, :] for ref in split_refs], axis=1
                ).astype(jnp.bfloat16)
                acc = acc + lax.dot_general(
                    vals, hot, (((1,), (1,)), ((), ())), preferred_element_type=jnp.float32
                )
    count = out_ref.shape[0]
    out_ref[:, 2] = jnp.broadcast_to(acc[0:1] + acc[1:2], (count, LANES))
    out_ref[:, 3] = jnp.broadcast_to(acc[2:3] + acc[3:4], (count, LANES))


def norm_kernel(scal_ref, d_ref, a_ref, out_ref):
    planes, rows, width = d_ref.shape
    _write_refs(scal_ref, d_ref, out_ref)
    for i, ref in enumerate((d_ref, a_ref)):
        acc = jnp.zeros((8, width), jnp.float32)
        for p in range(planes):
            for t in range((rows - 2 * PAD) // 8):
                v = ref[p, PAD + 8 * t : PAD + 8 * t + 8]
                acc = acc + v * v
        acc = sum(acc[:, LANES * j : LANES * (j + 1)] for j in range(width // LANES))
        out_ref[:, 2 + i] = jnp.broadcast_to(
            jnp.sum(acc, axis=0, keepdims=True), (out_ref.shape[0], LANES)
        )


def fields_kernel(scal_ref, recv_ref, d_ref, a_ref, ext_ref, own_ref, out_ref, sums_ref):
    planes, rows, width = d_ref.shape
    total = jnp.sum(recv_ref[...], axis=0)
    table = _table(total, 0)
    sums_ref[...] = jnp.broadcast_to(total[None, 2:4], sums_ref.shape)
    for p in range(planes):
        for t in range((rows - 2 * PAD) // 8):
            at = (p, slice(PAD + 8 * t, PAD + 8 * t + 8))
            to = (p, slice(8 * t, 8 * t + 8))
            own = own_ref[at]
            looked = jnp.concatenate(
                [_lookup(table, own[:, LANES * j : LANES * (j + 1)]) for j in range(width // LANES)],
                axis=1,
            )
            adjoint = a_ref[at]
            out_ref[(0,) + to] = adjoint * d_ref[at]
            out_ref[(1,) + to] = adjoint * (ext_ref[(3,) + at] * looked)


def on_device(rhs_direct, rhs_adjoint, diag_shift, flame_gain, ref_owner):
    planes, axial, radial = rhs_direct.shape
    sectors, blocks = lax.axis_size("sector"), lax.axis_size("block")
    core, block = lax.axis_index("flame"), lax.axis_index("block")
    scal = jnp.stack([core, block]).astype(jnp.int32)
    half, width, rows = planes // 2, 2 * radial, axial + 2 * PAD
    f32 = jnp.float32
    swap = [(0, 1), (1, 0)]

    stack = jnp.stack([rhs_direct, rhs_adjoint, diag_shift, flame_gain, ref_owner.astype(f32)])
    keep = lax.dynamic_slice_in_dim(stack, core * half, half, axis=1)
    give = lax.dynamic_slice_in_dim(stack, (1 - core) * half, half, axis=1)
    got = lax.ppermute(give, "flame", swap)
    full = jnp.where(
        core == 0, jnp.concatenate([keep, got], axis=3), jnp.concatenate([got, keep], axis=3)
    )
    before = lax.ppermute(full[:, :, axial - PAD :], "block", [(i, i + 1) for i in range(blocks - 1)])
    after = lax.ppermute(full[:, :, :PAD], "block", [(i + 1, i) for i in range(blocks - 1)])
    ext = jnp.concatenate([before, full, after], axis=2)

    field = jax.ShapeDtypeStruct((half, rows, width), f32)
    owners = jax.ShapeDtypeStruct((half, rows, width), jnp.int32)
    plane = jax.ShapeDtypeStruct((2, rows, width), f32)
    peers = 2 * blocks
    message = jax.ShapeDtypeStruct((peers, 4, LANES), f32)
    ring = [(2 * s, (2 * s - 1) % (2 * sectors)) for s in range(sectors)]
    ring += [(2 * s + 1, (2 * s + 2) % (2 * sectors)) for s in range(sectors)]

    inverse, owner, direct, adjoint, inner, outer = _call(
        functools.partial(init_kernel, blocks=blocks),
        (field, owners, field, field, plane, plane), 1, name="init",
    )(scal, ext)
    step = _call(step_kernel, (field, field, plane, plane), 8, name="step")
    collect = _call(
        collect_kernel, message, 4,
        [pltpu.VMEM((half * axial * 8, LANES), f32)] * (width // LANES), name="collect",
    )
    for _ in range(ITERS):
        outer_in = lax.ppermute(outer, ("sector", "flame"), ring)
        inner_in = lax.ppermute(inner, "flame", swap)
        sent = collect(scal, direct, adjoint, ext, owner)
        recv = lax.all_to_all(sent, BF, 0, 0, tiled=True)
        direct, adjoint, inner, outer = step(
            scal, recv, inner_in, outer_in, direct, adjoint, ext, inverse, owner
        )

    sent = _call(norm_kernel, message, 2, name="norm")(scal, direct, adjoint)
    recv = lax.all_to_all(sent, BF, 0, 0, tiled=True)
    fields, sums = _call(
        fields_kernel,
        (
            jax.ShapeDtypeStruct((2, half, axial, width), f32),
            jax.ShapeDtypeStruct((sectors, 2, LANES), f32),
        ),
        5, name="fields",
    )(scal, recv, direct, adjoint, ext, owner)
    keep = lax.dynamic_slice_in_dim(fields, core * radial, radial, axis=3)
    give = lax.dynamic_slice_in_dim(fields, (1 - core) * radial, radial, axis=3)
    got = lax.ppermute(give, "flame", swap)
    squares = lax.all_to_all(sums, "sector", 0, 0, tiled=True)
    squares = jnp.sum(squares, axis=(0, 2))
    cells = planes * axial * radial * sectors * blocks * 2
    scale = lax.rsqrt(squares[0] / cells * (squares[1] / cells) + 1e-12)
    low = jnp.where(core == 0, keep, got)
    high = jnp.where(core == 0, got, keep)
    out = jnp.concatenate([low, high], axis=1) * scale
    return out[0], out[1]


def solution(mesh):
    spec = P("sector", "block", "flame")
    return jax.shard_map(
        on_device,
        mesh=mesh,
        in_specs=(spec,) * 5,
        out_specs=(spec, spec),
        check_vma=False,
    )
```

```python
import functools

import jax
import jax.numpy as jnp
from jax import lax
from jax.experimental import pallas as pl
from jax.experimental.pallas import tpu as pltpu
from jax.sharding import PartitionSpec as P

ITERS = 6
REF_DEV = 8
PAD = 8
HALO = 6
LANES = 128
INTERPRET = False
BF = ("block", "flame")


def _call(kernel, out_shape, n_in, scratch=(), name=None):
    vmem = pl.BlockSpec(memory_space=pltpu.VMEM)
    single = not isinstance(out_shape, (tuple, list))
    return pl.pallas_call(
        kernel,
        out_shape=out_shape,
        in_specs=[pl.BlockSpec(memory_space=pltpu.SMEM)] + [vmem] * n_in,
        out_specs=vmem if single else [vmem] * len(out_shape),
        scratch_shapes=list(scratch),
        interpret=INTERPRET,
        name=name,
        compiler_params=pltpu.CompilerParams(vmem_limit_bytes=12 << 20),
    )


def _lookup(table, owner):
    low = jnp.take_along_axis(table[0], owner & (LANES - 1), axis=1, mode="promise_in_bounds")
    high = jnp.take_along_axis(table[1], owner & (LANES - 1), axis=1, mode="promise_in_bounds")
    return jnp.where(owner < LANES, low, high)


def _table(total, row):
    return [jnp.broadcast_to(total[row + j : row + j + 1], (8, LANES)) for j in (0, 1)]


def _send_planes(core, refs, inner_ref, outer_ref, planes):
    inner = jnp.where(core == 0, planes - 1, 0)
    for i, ref in enumerate(refs):
        inner_ref[i] = ref[inner]
        outer_ref[i] = ref[planes - 1 - inner]


def pack_kernel(scal_ref, *refs):
    core = scal_ref[0]
    ins, keep_ref, give_ref = refs[:-2], refs[-2], refs[-1]
    half = keep_ref.shape[1]
    for i, ref in enumerate(ins):
        for p in range(half):
            keep_ref[i, p] = ref[core * half + p].astype(jnp.float32)
            give_ref[i, p] = ref[(1 - core) * half + p].astype(jnp.float32)


def edges_kernel(scal_ref, keep_ref, got_ref, after_ref, before_ref):
    core = scal_ref[0]
    count, half, axial, radial = keep_ref.shape
    for i in range(count):
        for p in range(half):
            to = slice(p * HALO, (p + 1) * HALO)
            for ref, rng in ((after_ref, slice(0, HALO)), (before_ref, slice(axial - HALO, axial))):
                mine, other = keep_ref[i, p, rng], got_ref[i, p, rng]
                ref[i, to, :radial] = jnp.where(core == 0, mine, other)
                ref[i, to, radial:] = jnp.where(core == 0, other, mine)


def init_kernel(scal_ref, keep_ref, got_ref, before_ref, after_ref, bd_ref, ba_ref, gain_ref,
                inv_ref, own_ref, d_ref, a_ref, inner_ref, outer_ref, shift_ref, id_ref, *, blocks):
    core, block = scal_ref[0], scal_ref[1]
    _, half, axial, radial = keep_ref.shape
    rows = axial + 2 * PAD
    for i, ref in enumerate((bd_ref, ba_ref, shift_ref, gain_ref, id_ref)):
        for p in range(half):
            ref[p, :PAD] = jnp.zeros((PAD, 2 * radial), jnp.float32)
            ref[p, rows - PAD :] = jnp.zeros((PAD, 2 * radial), jnp.float32)
            ref[p, PAD - HALO : PAD] = before_ref[i, p * HALO : (p + 1) * HALO]
            ref[p, rows - PAD : rows - PAD + HALO] = after_ref[i, p * HALO : (p + 1) * HALO]
            mine, other = keep_ref[i, p], got_ref[i, p]
            ref[p, PAD : PAD + axial, :radial] = jnp.where(core == 0, mine, other)
            ref[p, PAD : PAD + axial, radial:] = jnp.where(core == 0, other, mine)
    for p in range(half):
        for t in range(rows // 8):
            at = (p, slice(8 * t, 8 * t + 8))
            inv = 1.0 / (6.0 + shift_ref[at])
            if t < PAD // 8:
                inv = jnp.where(block == 0, 0.0, inv)
            if t >= (rows - PAD) // 8:
                inv = jnp.where(block == blocks - 1, 0.0, inv)
            inv_ref[at] = inv
            own_ref[at] = id_ref[at].astype(jnp.int32)
            d_ref[at] = bd_ref[at] * inv
            a_ref[at] = ba_ref[at] * inv
    _send_planes(core, (d_ref, a_ref), inner_ref, outer_ref, half)


def step_kernel(scal_ref, *refs):
    dn_ref, an_ref, inner_out, outer_out = refs[-4:]
    _sweep(scal_ref, *refs[:-2])
    _send_planes(scal_ref[0], (dn_ref, an_ref), inner_out, outer_out, dn_ref.shape[0])


def _sweep(scal_ref, recv_ref, inner_ref, outer_ref, d_ref, a_ref, bd_ref, ba_ref, gain_ref,
           inv_ref, own_ref, dn_ref, an_ref):
    core, block = scal_ref[0], scal_ref[1]
    planes, rows, width = d_ref.shape
    tiles = rows // 8
    total = jnp.sum(recv_ref[...], axis=0)
    table = _table(total, 0)
    sums = _table(total, 2)
    lane = lax.broadcasted_iota(jnp.int32, (8, LANES), 1)
    sub = lax.broadcasted_iota(jnp.int32, (8, LANES), 0)
    spot = (lane % 32 == 0) & (sub == 0) & (core == 0)
    first = lax.broadcasted_iota(jnp.int32, (8, width), 1) == 0
    last = lax.broadcasted_iota(jnp.int32, (8, width), 1) == width - 1

    def source(blk):
        tab = jnp.where(blk < 8, sums[0], sums[1])
        parts = []
        for j in range(width // LANES):
            at = jnp.bitwise_and(blk, 7) * 16 + 4 * j + lane // 32
            got = jnp.take_along_axis(tab, at & (LANES - 1), axis=1, mode="promise_in_bounds")
            parts.append(jnp.where(spot, got, 0.0))
        return jnp.concatenate(parts, axis=1)

    def near(ref, field, p, t):
        rng = slice(8 * t, 8 * t + 8)
        here = ref[p, rng]
        if p == 0:
            below = jnp.where(core == 0, outer_ref[field, rng], inner_ref[field, rng])
        else:
            below = ref[p - 1, rng]
        if p == planes - 1:
            above = jnp.where(core == 0, inner_ref[field, rng], outer_ref[field, rng])
        else:
            above = ref[p + 1, rng]
        if t == 0:
            back = pltpu.roll(here, 1, 0)
        else:
            back = ref[p, 8 * t - 1 : 8 * t + 7]
        if t == tiles - 1:
            front = pltpu.roll(here, 7, 0)
        else:
            front = ref[p, 8 * t + 1 : 8 * t + 9]
        left = jnp.where(first, 0.0, pltpu.roll(here, 1, 1))
        right = jnp.where(last, 0.0, pltpu.roll(here, width - 1, 1))
        return (below + above) + (back + front) + (left + right)

    for p in range(planes):
        for t in range(tiles):
            at = (p, slice(8 * t, 8 * t + 8))
            inv = inv_ref[at]
            own = own_ref[at]
            looked = jnp.concatenate(
                [_lookup(table, own[:, LANES * j : LANES * (j + 1)]) for j in range(width // LANES)],
                axis=1,
            )
            flame = gain_ref[at] * looked
            dn_ref[at] = (bd_ref[at] + near(d_ref, 0, p, t) + flame) * inv
            acc = ba_ref[at] + near(a_ref, 1, p, t)
            if p == 0 and t == PAD // 8:
                acc = acc + source(block)
            if p == 0 and t == tiles - PAD // 8:
                acc = acc + source(block + 1)
            an_ref[at] = acc * inv


def _write_refs(scal_ref, d_ref, out_ref):
    core, block = scal_ref[0], scal_ref[1]
    width = d_ref.shape[2]
    lane = lax.broadcasted_iota(jnp.int32, (8, LANES), 1)
    row = d_ref[0, PAD : PAD + 8]
    got = jnp.zeros((8, LANES), jnp.float32)
    for j in range(width // LANES):
        part = jnp.broadcast_to(row[0:1, LANES * j : LANES * (j + 1)], (8, LANES))
        pick = jnp.take_along_axis(part, (lane & 3) * 32, axis=1, mode="promise_in_bounds")
        got = jnp.where((lane & 15) // 4 == j, pick, got)
    for half in (0, 1):
        mine = (lane // 16 + 8 * half == block) & (core == 0)
        out_ref[:, half] = jnp.broadcast_to(
            jnp.where(mine, got, 0.0)[0:1], (out_ref.shape[0], LANES)
        )


def collect_kernel(scal_ref, d_ref, a_ref, gain_ref, own_ref, out_ref, *split_refs):
    planes, rows, width = d_ref.shape
    tiles = (rows - 2 * PAD) // 8
    _write_refs(scal_ref, d_ref, out_ref)
    for p in range(planes):
        for t in range(tiles):
            at = (p, slice(PAD + 8 * t, PAD + 8 * t + 8))
            y = gain_ref[at] * a_ref[at]
            coarse = y.astype(jnp.bfloat16).astype(jnp.float32)
            fine = y - coarse
            upper = own_ref[at] >= LANES
            base = (p * tiles + t) * 64
            terms = (
                jnp.where(upper, 0.0, coarse),
                jnp.where(upper, 0.0, fine),
                jnp.where(upper, coarse, 0.0),
                jnp.where(upper, fine, 0.0),
            )
            for j in range(width // LANES):
                for k, term in enumerate(terms):
                    split_refs[j][pl.ds(base + k, 8, stride=8), :] = term[:, LANES * j : LANES * (j + 1)]
    ids = lax.broadcasted_iota(jnp.int32, (16, width), 0).astype(jnp.float32)
    one = jnp.ones((16, width), jnp.bfloat16)
    zero = jnp.zeros((16, width), jnp.bfloat16)
    groups = [(ids + 16.0 * g).astype(jnp.bfloat16) for g in range(LANES // 16)]
    acc = jnp.zeros((8, LANES), jnp.float32)
    for p in range(planes):
        for t in range(tiles):
            low = (own_ref[p, PAD + 8 * t : PAD + 8 * t + 8] & (LANES - 1)).astype(jnp.float32)
            for x in range(8):
                line = jnp.broadcast_to(low[x : x + 1], (16, width)).astype(jnp.bfloat16)
                hot = jnp.concatenate([jnp.where(line == g, one, zero) for g in groups], axis=0)
                base = ((p * tiles + t) * 8 + x) * 8
                vals = jnp.concatenate(
                    [ref[base : base + 8, :] for ref in split_refs], axis=1
                ).astype(jnp.bfloat16)
                acc = acc + lax.dot_general(
                    vals, hot, (((1,), (1,)), ((), ())), preferred_element_type=jnp.float32
                )
    count = out_ref.shape[0]
    out_ref[:, 2] = jnp.broadcast_to(acc[0:1] + acc[1:2], (count, LANES))
    out_ref[:, 3] = jnp.broadcast_to(acc[2:3] + acc[3:4], (count, LANES))


def last_kernel(scal_ref, *refs):
    ins, (keep_ref, give_ref, out_ref, dn_ref, an_ref) = refs[:-5], refs[-5:]
    core = scal_ref[0]
    _sweep(scal_ref, *ins, dn_ref, an_ref)
    _write_refs(scal_ref, dn_ref, out_ref)
    planes, rows, width = dn_ref.shape
    radial = width // 2
    for i, ref in enumerate((dn_ref, an_ref)):
        acc = jnp.zeros((8, width), jnp.float32)
        for p in range(planes):
            for t in range((rows - 2 * PAD) // 8):
                v = ref[p, PAD + 8 * t : PAD + 8 * t + 8]
                acc = acc + v * v
                low, high = v[:, :radial], v[:, radial:]
                keep_ref[i, p, 8 * t : 8 * t + 8] = jnp.where(core == 0, low, high)
                give_ref[i, p, 8 * t : 8 * t + 8] = jnp.where(core == 0, high, low)
        acc = sum(acc[:, LANES * j : LANES * (j + 1)] for j in range(width // LANES))
        out_ref[:, 2 + i] = jnp.broadcast_to(
            jnp.sum(acc, axis=0, keepdims=True), (out_ref.shape[0], LANES)
        )


def squares_kernel(scal_ref, recv_ref, out_ref):
    out_ref[...] = jnp.broadcast_to(
        jnp.sum(recv_ref[...], axis=0)[None, 2:4], out_ref.shape
    )


def fields_kernel(scal_ref, recv_ref, squares_ref, keep_ref, got_ref, gain_ref, own_ref,
                  first_ref, second_ref, *, cells):
    core = scal_ref[0]
    planes, axial, radial = gain_ref.shape
    half = planes // 2
    table = _table(jnp.sum(recv_ref[...], axis=0), 0)
    squares = jnp.sum(jnp.sum(squares_ref[...], axis=0), axis=1, keepdims=True) / cells
    scale = lax.rsqrt(squares[0:1] * squares[1:2] + 1e-12)
    for p in range(planes):
        for t in range(axial // 8):
            rng = slice(8 * t, 8 * t + 8)
            mine = core == 0 if p < half else core == 1
            direct, adjoint = (
                jnp.where(mine, keep_ref[i, p % half, rng], got_ref[i, p % half, rng]) for i in (0, 1)
            )
            own = own_ref[p, rng]
            looked = jnp.concatenate(
                [_lookup(table, own[:, LANES * j : LANES * (j + 1)]) for j in range(radial // LANES)],
                axis=1,
            )
            first_ref[p, rng] = adjoint * direct * scale
            second_ref[p, rng] = adjoint * (gain_ref[p, rng] * looked) * scale


def on_device(rhs_direct, rhs_adjoint, diag_shift, flame_gain, ref_owner):
    planes, axial, radial = rhs_direct.shape
    sectors, blocks = lax.axis_size("sector"), lax.axis_size("block")
    core, block = lax.axis_index("flame"), lax.axis_index("block")
    scal = jnp.stack([core, block]).astype(jnp.int32)
    half, width, rows = planes // 2, 2 * radial, axial + 2 * PAD
    swap = [(0, 1), (1, 0)]
    ring = [(2 * s, (2 * s - 1) % (2 * sectors)) for s in range(sectors)]
    ring += [(2 * s + 1, (2 * s + 2) % (2 * sectors)) for s in range(sectors)]

    def arr(*shape, dtype=jnp.float32):
        return jax.ShapeDtypeStruct(shape, dtype)

    quarter = arr(5, half, axial, radial)
    keep, give = _call(pack_kernel, (quarter, quarter), 5, name="pack")(
        scal, rhs_direct, rhs_adjoint, diag_shift, flame_gain, ref_owner
    )
    got = lax.ppermute(give, "flame", swap)
    edge = arr(5, half * HALO, width)
    first_rows, last_rows = _call(edges_kernel, (edge, edge), 2, name="edges")(scal, keep, got)
    before = lax.ppermute(last_rows, "block", [(i, i + 1) for i in range(blocks - 1)])
    after = lax.ppermute(first_rows, "block", [(i + 1, i) for i in range(blocks - 1)])

    field, plane = arr(half, rows, width), arr(2, rows, width)
    message = arr(2 * blocks, 4, LANES)
    bd, ba, gain, inverse, owner, direct, adjoint, inner, outer = _call(
        functools.partial(init_kernel, blocks=blocks),
        (field,) * 4 + (arr(half, rows, width, dtype=jnp.int32), field, field, plane, plane),
        4, [pltpu.VMEM((half, rows, width), jnp.float32)] * 2, name="init",
    )(scal, keep, got, before, after)
    step = _call(step_kernel, (field, field, plane, plane), 10, name="step")
    last = _call(
        last_kernel, (arr(2, half, axial, radial), arr(2, half, axial, radial), message), 10,
        [pltpu.VMEM((half, rows, width), jnp.float32)] * 2, name="last",
    )
    collect = _call(
        collect_kernel, message, 4,
        [pltpu.VMEM((half * axial * 8, LANES), jnp.float32)] * (width // LANES), name="collect",
    )
    for sweep in range(ITERS):
        outer_in = lax.ppermute(outer, ("sector", "flame"), ring)
        inner_in = lax.ppermute(inner, "flame", swap)
        sent = collect(scal, direct, adjoint, gain, owner)
        recv = lax.all_to_all(sent, BF, 0, 0, tiled=True)
        args = (scal, recv, inner_in, outer_in, direct, adjoint, bd, ba, gain, inverse, owner)
        if sweep < ITERS - 1:
            direct, adjoint, inner, outer = step(*args)
        else:
            keep, give, sent = last(*args)

    got = lax.ppermute(give, "flame", swap)
    recv = lax.all_to_all(sent, BF, 0, 0, tiled=True)
    squares = _call(squares_kernel, arr(sectors, 2, LANES), 1, name="squares")(scal, recv)
    squares = lax.all_to_all(squares, "sector", 0, 0, tiled=True)
    out = arr(planes, axial, radial)
    cells = planes * axial * radial * sectors * blocks * 2
    return tuple(
        _call(functools.partial(fields_kernel, cells=cells), (out, out), 6, name="fields")(
            scal, recv, squares, keep, got, flame_gain, ref_owner
        )
    )


def solution(mesh):
    spec = P("sector", "block", "flame")
    return jax.shard_map(
        on_device,
        mesh=mesh,
        in_specs=(spec,) * 5,
        out_specs=(spec, spec),
        check_vma=False,
    )
```

```python
import functools

import jax
import jax.numpy as jnp
from jax import lax
from jax.experimental import pallas as pl
from jax.experimental.pallas import tpu as pltpu
from jax.sharding import PartitionSpec as P

ITERS = 6
REF_DEV = 8
PAD = 8
HALO = 6
LANES = 128
INTERPRET = False
BF = ("block", "flame")


def _call(kernel, out_shape, n_in, scratch=(), name=None, space=pltpu.VMEM):
    vmem = pl.BlockSpec(memory_space=pltpu.VMEM)
    single = not isinstance(out_shape, (tuple, list))
    return pl.pallas_call(
        kernel,
        out_shape=out_shape,
        in_specs=[pl.BlockSpec(memory_space=pltpu.SMEM)] + [pl.BlockSpec(memory_space=space)] * n_in,
        out_specs=vmem if single else [vmem] * len(out_shape),
        scratch_shapes=list(scratch),
        interpret=INTERPRET,
        name=name,
        compiler_params=pltpu.CompilerParams(vmem_limit_bytes=24 << 20),
    )


def _lookup(table, owner):
    low = jnp.take_along_axis(table[0], owner & (LANES - 1), axis=1, mode="promise_in_bounds")
    high = jnp.take_along_axis(table[1], owner & (LANES - 1), axis=1, mode="promise_in_bounds")
    return jnp.where(owner < LANES, low, high)


def _table(total, row):
    return [jnp.broadcast_to(total[row + j : row + j + 1], (8, LANES)) for j in (0, 1)]


def _send_planes(refs, inner_ref, outer_ref):
    for i, ref in enumerate(refs):
        inner_ref[i] = ref[ref.shape[0] - 1]
        outer_ref[i] = ref[0]


def pack_kernel(scal_ref, *refs):
    core = scal_ref[0]
    ins, (keep_ref, give_ref, keep_id, give_id, sems) = refs[:5], refs[5:]
    half = keep_ref.shape[1]
    copies = []
    for i, ref in enumerate(ins):
        for p in range(half):
            step = 2 * half - 1 - 2 * p
            for k, (dst, ids, at) in enumerate(
                ((keep_ref, keep_id, core), (give_ref, give_id, 1 - core))
            ):
                to = dst.at[i, p] if i < 4 else ids.at[p]
                copies.append(pltpu.make_async_copy(ref.at[p + at * step], to, sems.at[i, p, k]))
    for copy in copies:
        copy.start()
    for copy in copies:
        copy.wait()
    keep_ref[4] = keep_id[...].astype(jnp.float32)
    give_ref[4] = give_id[...].astype(jnp.float32)


def edges_kernel(scal_ref, keep_ref, got_ref, after_ref, before_ref):
    core = scal_ref[0]
    count, half, axial, radial = keep_ref.shape
    for i in range(count):
        for p in range(half):
            to = slice(p * HALO, (p + 1) * HALO)
            for ref, rng in ((after_ref, slice(0, HALO)), (before_ref, slice(axial - HALO, axial))):
                mine, other = keep_ref[i, p, rng], got_ref[i, p, rng]
                ref[i, to, :radial] = jnp.where(core == 0, mine, other)
                ref[i, to, radial:] = jnp.where(core == 0, other, mine)


def init_kernel(scal_ref, keep_ref, got_ref, before_ref, after_ref, bd_ref, ba_ref, gain_ref,
                inv_ref, own_ref, hot_ref, d_ref, a_ref, inner_ref, outer_ref, out_ref,
                shift_ref, id_ref, *split_refs, blocks):
    core, block = scal_ref[0], scal_ref[1]
    _, half, axial, radial = keep_ref.shape
    rows = axial + 2 * PAD
    for i, ref in enumerate((bd_ref, ba_ref, shift_ref, gain_ref, id_ref)):
        for p in range(half):
            ref[p, :PAD] = jnp.zeros((PAD, 2 * radial), jnp.float32)
            ref[p, rows - PAD :] = jnp.zeros((PAD, 2 * radial), jnp.float32)
            ref[p, PAD - HALO : PAD] = before_ref[i, p * HALO : (p + 1) * HALO]
            ref[p, rows - PAD : rows - PAD + HALO] = after_ref[i, p * HALO : (p + 1) * HALO]
            mine, other = keep_ref[i, p], got_ref[i, p]
            ref[p, PAD : PAD + axial, :radial] = jnp.where(core == 0, mine, other)
            ref[p, PAD : PAD + axial, radial:] = jnp.where(core == 0, other, mine)
    for p in range(half):
        for t in range(rows // 8):
            at = (p, slice(8 * t, 8 * t + 8))
            inv = 1.0 / (6.0 + shift_ref[at])
            if t < PAD // 8:
                inv = jnp.where(block == 0, 0.0, inv)
            if t >= (rows - PAD) // 8:
                inv = jnp.where(block == blocks - 1, 0.0, inv)
            inv_ref[at] = inv
            own_ref[at] = id_ref[at].astype(jnp.int32)
            d_ref[at] = bd_ref[at] * inv
            a_ref[at] = ba_ref[at] * inv
    _send_planes((d_ref, a_ref), inner_ref, outer_ref)
    width = 2 * radial
    ids = lax.broadcasted_iota(jnp.int32, (16, width), 0).astype(jnp.float32)
    one = jnp.ones((16, width), jnp.bfloat16)
    zero = jnp.zeros((16, width), jnp.bfloat16)
    for p in range(half):
        for t in range(axial // 8):
            low = (own_ref[p, PAD + 8 * t : PAD + 8 * t + 8] & (LANES - 1)).astype(jnp.float32)
            for x in range(8):
                line = jnp.broadcast_to(low[x : x + 1], (16, width)).astype(jnp.bfloat16)
                for g in range(LANES // 16):
                    hit = line == (ids + 16.0 * g).astype(jnp.bfloat16)
                    hot_ref[(p * (axial // 8) + t) * 8 + x, 16 * g : 16 * g + 16] = jnp.where(hit, one, zero)
    _collect(scal_ref, d_ref, a_ref, gain_ref, own_ref, hot_ref, out_ref, split_refs)


def step_kernel(scal_ref, *refs):
    ins, hot_ref, refs = refs[:10], refs[10], refs[11:]
    (dn_ref, an_ref, inner_out, outer_out, out_ref), split_refs = refs[:5], refs[5:]
    _sweep(scal_ref, *ins, dn_ref, an_ref)
    _send_planes((dn_ref, an_ref), inner_out, outer_out)
    _collect(scal_ref, dn_ref, an_ref, ins[7], ins[9], hot_ref, out_ref, split_refs)


def _sweep(scal_ref, recv_ref, inner_ref, outer_ref, d_ref, a_ref, bd_ref, ba_ref, gain_ref,
           inv_ref, own_ref, dn_ref, an_ref):
    core, block = scal_ref[0], scal_ref[1]
    planes, rows, width = d_ref.shape
    tiles = rows // 8
    total = jnp.sum(recv_ref[...], axis=0)
    table = _table(total, 0)
    sums = _table(total, 2)
    lane = lax.broadcasted_iota(jnp.int32, (8, LANES), 1)
    sub = lax.broadcasted_iota(jnp.int32, (8, LANES), 0)
    spot = (lane % 32 == 0) & (sub == 0) & (core == 0)
    first = lax.broadcasted_iota(jnp.int32, (8, width), 1) == 0
    last = lax.broadcasted_iota(jnp.int32, (8, width), 1) == width - 1

    def source(blk):
        tab = jnp.where(blk < 8, sums[0], sums[1])
        parts = []
        for j in range(width // LANES):
            at = jnp.bitwise_and(blk, 7) * 16 + 4 * j + lane // 32
            got = jnp.take_along_axis(tab, at & (LANES - 1), axis=1, mode="promise_in_bounds")
            parts.append(jnp.where(spot, got, 0.0))
        return jnp.concatenate(parts, axis=1)

    def near(ref, field, p, t):
        rng = slice(8 * t, 8 * t + 8)
        here = ref[p, rng]
        below = outer_ref[field, rng] if p == 0 else ref[p - 1, rng]
        above = inner_ref[field, rng] if p == planes - 1 else ref[p + 1, rng]
        if t == 0:
            back = pltpu.roll(here, 1, 0)
        else:
            back = ref[p, 8 * t - 1 : 8 * t + 7]
        if t == tiles - 1:
            front = pltpu.roll(here, 7, 0)
        else:
            front = ref[p, 8 * t + 1 : 8 * t + 9]
        left = jnp.where(first, 0.0, pltpu.roll(here, 1, 1))
        right = jnp.where(last, 0.0, pltpu.roll(here, width - 1, 1))
        return (below + above) + (back + front) + (left + right)

    for p in range(planes):
        for t in range(tiles):
            at = (p, slice(8 * t, 8 * t + 8))
            inv = inv_ref[at]
            own = own_ref[at]
            looked = jnp.concatenate(
                [_lookup(table, own[:, LANES * j : LANES * (j + 1)]) for j in range(width // LANES)],
                axis=1,
            )
            flame = gain_ref[at] * looked
            dn_ref[at] = (bd_ref[at] + near(d_ref, 0, p, t) + flame) * inv
            acc = ba_ref[at] + near(a_ref, 1, p, t)
            if p == 0 and t == PAD // 8:
                acc = acc + source(block)
            if p == 0 and t == tiles - PAD // 8:
                acc = acc + source(block + 1)
            an_ref[at] = acc * inv


def _ref_values(d_ref):
    width = d_ref.shape[2]
    lane = lax.broadcasted_iota(jnp.int32, (8, LANES), 1)
    row = d_ref[0, PAD : PAD + 8]
    got = jnp.zeros((8, LANES), jnp.float32)
    for j in range(width // LANES):
        part = jnp.broadcast_to(row[0:1, LANES * j : LANES * (j + 1)], (8, LANES))
        pick = jnp.take_along_axis(part, (lane & 3) * 32, axis=1, mode="promise_in_bounds")
        got = jnp.where((lane & 15) // 4 == j, pick, got)
    return lane, got


def _write_refs(scal_ref, d_ref, out_ref):
    core, block = scal_ref[0], scal_ref[1]
    lane, got = _ref_values(d_ref)
    for half in (0, 1):
        mine = (lane // 16 + 8 * half == block) & (core == 0)
        out_ref[:, half] = jnp.broadcast_to(
            jnp.where(mine, got, 0.0)[0:1], (out_ref.shape[0], LANES)
        )


def _collect(scal_ref, d_ref, a_ref, gain_ref, own_ref, hot_ref, out_ref, split_refs):
    planes, rows, width = d_ref.shape
    tiles = (rows - 2 * PAD) // 8
    _write_refs(scal_ref, d_ref, out_ref)
    for p in range(planes):
        for t in range(tiles):
            at = (p, slice(PAD + 8 * t, PAD + 8 * t + 8))
            y = gain_ref[at] * a_ref[at]
            coarse = y.astype(jnp.bfloat16).astype(jnp.float32)
            fine = y - coarse
            upper = own_ref[at] >= LANES
            base = (p * tiles + t) * 64
            terms = (
                jnp.where(upper, 0.0, coarse),
                jnp.where(upper, 0.0, fine),
                jnp.where(upper, coarse, 0.0),
                jnp.where(upper, fine, 0.0),
            )
            for j in range(width // LANES):
                for k, term in enumerate(terms):
                    split_refs[j][pl.ds(base + k, 8, stride=8), :] = term[:, LANES * j : LANES * (j + 1)]
    acc = jnp.zeros((8, LANES), jnp.float32)
    for line in range(hot_ref.shape[0]):
        vals = jnp.concatenate([ref[8 * line : 8 * line + 8, :] for ref in split_refs], axis=1)
        acc = acc + lax.dot_general(
            vals.astype(jnp.bfloat16), hot_ref[line], (((1,), (1,)), ((), ())),
            preferred_element_type=jnp.float32,
        )
    count = out_ref.shape[0]
    out_ref[:, 2] = jnp.broadcast_to(acc[0:1] + acc[1:2], (count, LANES))
    out_ref[:, 3] = jnp.broadcast_to(acc[2:3] + acc[3:4], (count, LANES))


def last_kernel(scal_ref, *refs):
    ins, (keep_ref, give_ref, out_ref, dn_ref, an_ref) = refs[:-5], refs[-5:]
    core, block = scal_ref[0], scal_ref[1]
    _sweep(scal_ref, *ins, dn_ref, an_ref)
    planes, rows, width = dn_ref.shape
    radial = width // 2
    lane, values = _ref_values(dn_ref)
    line = jnp.where((lane // 16 == jnp.bitwise_and(block, 3)) & (core == 0), values, 0.0)[0:1]
    for i, ref in enumerate((dn_ref, an_ref)):
        acc = jnp.zeros((8, width), jnp.float32)
        for p in range(planes):
            for t in range((rows - 2 * PAD) // 8):
                v = ref[p, PAD + 8 * t : PAD + 8 * t + 8]
                acc = acc + v * v
                low, high = v[:, :radial], v[:, radial:]
                keep_ref[i, p, 8 * t : 8 * t + 8] = jnp.where(core == 0, low, high)
                give_ref[i, p, 8 * t : 8 * t + 8] = jnp.where(core == 0, high, low)
        acc = sum(acc[:, LANES * j : LANES * (j + 1)] for j in range(width // LANES))
        acc = acc + pltpu.roll(acc, 64, 1)
        acc = jnp.sum(acc + pltpu.roll(acc, 32, 1), axis=0, keepdims=True)
        line = jnp.where(lane[0:1] // 32 == 2 + i, acc, line)
    out_ref[...] = jnp.broadcast_to(line, out_ref.shape)


def fields_kernel(scal_ref, recv_ref, keep_ref, got_ref, gain_ref, own_ref, first_ref, second_ref,
                  *, cells, group):
    core, sector = scal_ref[0], scal_ref[2]
    planes, axial, radial = gain_ref.shape
    half = planes // 2
    lane = lax.broadcasted_iota(jnp.int32, (8, LANES), 1)
    quads = [
        jnp.broadcast_to(
            jnp.sum(recv_ref[pl.ds(pl.multiple_of(sector * group, 8) + 8 * j, 8), :], axis=0, keepdims=True),
            (8, LANES),
        )
        for j in range(4)
    ]
    table = [jnp.where(lane < 64, quads[2 * j], pltpu.roll(quads[2 * j + 1], 64, 1)) for j in (0, 1)]
    total = jnp.broadcast_to(jnp.sum(recv_ref[...], axis=0, keepdims=True), (8, LANES))
    squares = [
        jnp.sum(jnp.where(lane // 32 == 2 + i, total, 0.0), axis=1, keepdims=True)[0:1] / cells
        for i in (0, 1)
    ]
    scale = lax.rsqrt(squares[0] * squares[1] + 1e-12)
    for p in range(planes):
        for t in range(axial // 8):
            rng = slice(8 * t, 8 * t + 8)
            mine, at = (core == 0, p) if p < half else (core == 1, planes - 1 - p)
            direct, adjoint = (
                jnp.where(mine, keep_ref[i, at, rng], got_ref[i, at, rng]) for i in (0, 1)
            )
            own = own_ref[p, rng]
            looked = jnp.concatenate(
                [_lookup(table, own[:, LANES * j : LANES * (j + 1)]) for j in range(radial // LANES)],
                axis=1,
            )
            first_ref[p, rng] = adjoint * direct * scale
            second_ref[p, rng] = adjoint * (gain_ref[p, rng] * looked) * scale


def on_device(rhs_direct, rhs_adjoint, diag_shift, flame_gain, ref_owner):
    planes, axial, radial = rhs_direct.shape
    sectors, blocks = lax.axis_size("sector"), lax.axis_size("block")
    core, block = lax.axis_index("flame"), lax.axis_index("block")
    scal = jnp.stack([core, block, lax.axis_index("sector")]).astype(jnp.int32)
    half, width, rows = planes // 2, 2 * radial, axial + 2 * PAD
    swap = [(0, 1), (1, 0)]
    ring = [(2 * s, (2 * s - 1) % (2 * sectors)) for s in range(sectors)]
    ring += [(2 * s + 1, (2 * s + 2) % (2 * sectors)) for s in range(sectors)]

    def arr(*shape, dtype=jnp.float32):
        return jax.ShapeDtypeStruct(shape, dtype)

    quarter = arr(5, half, axial, radial)
    ids = pltpu.VMEM((half, axial, radial), jnp.int32)
    keep, give = _call(
        pack_kernel, (quarter, quarter), 5, [ids, ids, pltpu.SemaphoreType.DMA((5, half, 2))],
        name="pack", space=pltpu.HBM,
    )(scal, rhs_direct, rhs_adjoint, diag_shift, flame_gain, ref_owner)
    got = lax.ppermute(give, "flame", swap)
    edge = arr(5, half * HALO, width)
    first_rows, last_rows = _call(edges_kernel, (edge, edge), 2, name="edges")(scal, keep, got)
    before = lax.ppermute(last_rows, "block", [(i, i + 1) for i in range(blocks - 1)])
    after = lax.ppermute(first_rows, "block", [(i + 1, i) for i in range(blocks - 1)])

    field, plane = arr(half, rows, width), arr(2, rows, width)
    full = pltpu.VMEM((half, rows, width), jnp.float32)
    split = [pltpu.VMEM((half * axial * 8, LANES), jnp.float32)] * (width // LANES)
    moving = (field, field, plane, plane, arr(2 * blocks, 4, LANES))
    owners = arr(half, rows, width, dtype=jnp.int32)
    hot = arr(half * axial, LANES, width, dtype=jnp.bfloat16)
    bd, ba, gain, inverse, owner, hot, direct, adjoint, inner, outer, sent = _call(
        functools.partial(init_kernel, blocks=blocks),
        (field, field, field, field, owners, hot) + moving, 4, [full, full] + split, name="init",
    )(scal, keep, got, before, after)
    step = _call(step_kernel, moving, 11, split, name="step")
    cut = arr(2, half, axial, radial)
    everyone = 2 * blocks * sectors
    last = _call(last_kernel, (cut, cut, arr(everyone, LANES)), 10, [full, full], name="last")
    for sweep in range(ITERS):
        outer_in = lax.ppermute(outer, ("sector", "flame"), ring)
        inner_in = lax.ppermute(inner, "flame", swap)
        recv = lax.all_to_all(sent, BF, 0, 0, tiled=True)
        args = (scal, recv, inner_in, outer_in, direct, adjoint, bd, ba, gain, inverse, owner)
        if sweep < ITERS - 1:
            direct, adjoint, inner, outer, sent = step(*args, hot)
        else:
            keep, give, sent = last(*args)

    got = lax.ppermute(give, "flame", swap)
    recv = lax.all_to_all(sent, ("sector",) + BF, 0, 0, tiled=True)
    out = arr(planes, axial, radial)
    cells = planes * axial * radial * everyone
    return tuple(
        _call(
            functools.partial(fields_kernel, cells=cells, group=2 * blocks), (out, out), 5, name="fields"
        )(scal, recv, keep, got, flame_gain, ref_owner)
    )


def solution(mesh):
    spec = P("sector", "block", "flame")
    return jax.shard_map(
        on_device,
        mesh=mesh,
        in_specs=(spec,) * 5,
        out_specs=(spec, spec),
        check_vma=False,
    )
```

```python
import functools

import jax
import jax.numpy as jnp
from jax import lax
from jax.experimental import pallas as pl
from jax.experimental.pallas import tpu as pltpu
from jax.sharding import PartitionSpec as P

ITERS = 6
REF_DEV = 8
INNER = 3
PAD = 8
HALO = 6
LANES = 128
INTERPRET = False
BF = ("block", "flame")


def _call(kernel, out_shape, n_in, scratch=(), name=None, space=pltpu.VMEM):
    vmem = pl.BlockSpec(memory_space=pltpu.VMEM)
    single = not isinstance(out_shape, (tuple, list))
    call = pl.pallas_call(
        kernel,
        out_shape=out_shape,
        in_specs=[pl.BlockSpec(memory_space=pltpu.SMEM)] + [pl.BlockSpec(memory_space=space)] * n_in,
        out_specs=vmem if single else [vmem] * len(out_shape),
        scratch_shapes=list(scratch),
        interpret=INTERPRET,
        name=name,
        compiler_params=pltpu.CompilerParams(vmem_limit_bytes=24 << 20),
    )
    if space is pltpu.VMEM or INTERPRET:
        return call
    return lambda scal, *args: call(
        scal, *(pltpu.with_memory_space_constraint(x, space) for x in args)
    )


def _lookup(table, owner):
    low = jnp.take_along_axis(table[0], owner & (LANES - 1), axis=1, mode="promise_in_bounds")
    high = jnp.take_along_axis(table[1], owner & (LANES - 1), axis=1, mode="promise_in_bounds")
    return jnp.where(owner < LANES, low, high)


def _table(total, row):
    return [jnp.broadcast_to(total[row + j : row + j + 1], (8, LANES)) for j in (0, 1)]


def pack_kernel(scal_ref, *refs):
    core = scal_ref[0]
    ins, (keep_ref, give_ref, keep_id, give_id, sems) = refs[:5], refs[5:]
    half = keep_ref.shape[1]
    copies = []
    for i, ref in enumerate(ins):
        for p in range(half):
            step = 2 * half - 1 - 2 * p
            for k, (dst, ids, at) in enumerate(
                ((keep_ref, keep_id, core), (give_ref, give_id, 1 - core))
            ):
                to = dst.at[i, p] if i < 4 else ids.at[p]
                copies.append(pltpu.make_async_copy(ref.at[p + at * step], to, sems.at[i, p, k]))
    for copy in copies:
        copy.start()
    for copy in copies:
        copy.wait()
    keep_ref[4] = keep_id[...].astype(jnp.float32)
    give_ref[4] = give_id[...].astype(jnp.float32)


def edges_kernel(scal_ref, keep_ref, got_ref, after_ref, before_ref):
    core = scal_ref[0]
    count, half, axial, radial = keep_ref.shape
    for i in range(count):
        for p in range(half):
            to = slice(p * HALO, (p + 1) * HALO)
            for ref, rng in ((after_ref, slice(0, HALO)), (before_ref, slice(axial - HALO, axial))):
                mine, other = keep_ref[i, p, rng], got_ref[i, p, rng]
                ref[i, to, :radial] = jnp.where(core == 0, mine, other)
                ref[i, to, radial:] = jnp.where(core == 0, other, mine)


def hot_kernel(scal_ref, keep_ref, got_ref, hot_ref):
    core = scal_ref[0]
    count, half, axial, radial = keep_ref.shape
    ids = lax.broadcasted_iota(jnp.int32, (16, radial), 0).astype(jnp.float32)
    one = jnp.ones((16, radial), jnp.bfloat16)
    zero = jnp.zeros((16, radial), jnp.bfloat16)
    groups = [(ids + 16.0 * g).astype(jnp.bfloat16) for g in range(LANES // 16)]
    for p in range(half):
        for t in range(axial // 8):
            mine, other = (r[count - 1, p, 8 * t : 8 * t + 8] for r in (keep_ref, got_ref))
            for h in (0, 1):
                owner = jnp.where(core == h, mine, other)
                low = jnp.where(owner >= LANES, owner - LANES, owner)
                for x in range(8):
                    line = jnp.broadcast_to(low[x : x + 1], (16, radial)).astype(jnp.bfloat16)
                    for g, group in enumerate(groups):
                        hot_ref[
                            (p * (axial // 8) + t) * 8 + x, 16 * g : 16 * g + 16,
                            radial * h : radial * (h + 1),
                        ] = jnp.where(line == group, one, zero)


def init_kernel(scal_ref, keep_ref, got_ref, before_ref, after_ref, hot_ref, bd_ref, ba_ref, gain_ref,
                inv_ref, own_ref, d_ref, a_ref, inner_ref, outer_ref, out_ref,
                shift_ref, id_ref, *split_refs, blocks):
    core, block = scal_ref[0], scal_ref[1]
    _, half, axial, radial = keep_ref.shape
    rows = axial + 2 * PAD
    for i, ref in enumerate((bd_ref, ba_ref, shift_ref, gain_ref, id_ref)):
        for p in range(half):
            ref[p, :PAD] = jnp.zeros((PAD, 2 * radial), jnp.float32)
            ref[p, rows - PAD :] = jnp.zeros((PAD, 2 * radial), jnp.float32)
            ref[p, PAD - HALO : PAD] = before_ref[i, p * HALO : (p + 1) * HALO]
            ref[p, rows - PAD : rows - PAD + HALO] = after_ref[i, p * HALO : (p + 1) * HALO]
            mine, other = keep_ref[i, p], got_ref[i, p]
            ref[p, PAD : PAD + axial, :radial] = jnp.where(core == 0, mine, other)
            ref[p, PAD : PAD + axial, radial:] = jnp.where(core == 0, other, mine)
    for p in range(half):
        for t in range(rows // 8):
            at = (p, slice(8 * t, 8 * t + 8))
            inv = 1.0 / (6.0 + shift_ref[at])
            if t < PAD // 8:
                inv = jnp.where(block == 0, 0.0, inv)
            if t >= (rows - PAD) // 8:
                inv = jnp.where(block == blocks - 1, 0.0, inv)
            inv_ref[at] = inv
            own_ref[at] = id_ref[at].astype(jnp.int32)
            d_ref[at] = bd_ref[at] * inv
            a_ref[at] = ba_ref[at] * inv
    for i, ref in enumerate((bd_ref, ba_ref, inv_ref, gain_ref, id_ref)):
        for depth in range(INNER):
            inner_ref[i, depth] = ref[half - 1 - depth]
    _send(outer_ref, d_ref, a_ref)
    _collect(scal_ref, d_ref, a_ref, gain_ref, own_ref, hot_ref, out_ref, split_refs)


def _send(outer_ref, d_ref, a_ref):
    outer_ref[0] = d_ref[0]
    outer_ref[1] = a_ref[0]


def step_kernel(scal_ref, *refs, extra, first):
    refs = list(refs)
    ins = [refs.pop(0) for _ in range(10)]
    halo_ref = None if first else refs.pop(0)
    hot_ref = refs.pop(0)
    dn_ref, an_ref, hn_ref, outer_ref, out_ref = [refs.pop(0) for _ in range(5)]
    if first:
        halo_ref = refs.pop(0)
        for i in (0, 1):
            for depth in range(INNER):
                halo_ref[i, depth] = ins[9][i, depth] * ins[9][2, depth]
    _sweep(scal_ref, *ins, halo_ref, dn_ref, an_ref, hn_ref, extra)
    if not extra:
        for i, ref in enumerate((dn_ref, an_ref)):
            for depth in range(INNER):
                hn_ref[i, depth] = ref[ref.shape[0] - 1 - depth]
    _send(outer_ref, dn_ref, an_ref)
    _collect(scal_ref, dn_ref, an_ref, ins[6], ins[8], hot_ref, out_ref, refs)


def _sweep(scal_ref, recv_ref, outer_ref, d_ref, a_ref, bd_ref, ba_ref, gain_ref,
           inv_ref, own_ref, deep_ref, halo_ref, dn_ref, an_ref, hn_ref, extra, pad=0):
    core, block = scal_ref[0], scal_ref[1]
    planes, rows, width = d_ref.shape
    tiles = rows // 8
    total = jnp.sum(recv_ref[...], axis=0)
    table = _table(total, 0)
    sums = _table(total, 2)
    lane = lax.broadcasted_iota(jnp.int32, (8, LANES), 1)
    sub = lax.broadcasted_iota(jnp.int32, (8, LANES), 0)
    spot = (lane % 32 == 0) & (sub == 0) & (core == 0)
    first = lax.broadcasted_iota(jnp.int32, (8, width), 1) == 0
    last = lax.broadcasted_iota(jnp.int32, (8, width), 1) == width - 1

    def source(blk):
        tab = jnp.where(blk < 8, sums[0], sums[1])
        parts = []
        for j in range(width // LANES):
            at = jnp.bitwise_and(blk, 7) * 16 + 4 * j + lane // 32
            got = jnp.take_along_axis(tab, at & (LANES - 1), axis=1, mode="promise_in_bounds")
            parts.append(jnp.where(spot, got, 0.0))
        return jnp.concatenate(parts, axis=1)

    def plane(ref, field, p, rng):
        if p < 0:
            return outer_ref[field, rng]
        return ref[p, rng] if p < planes else halo_ref[field, p - planes, rng]

    def near(ref, field, p, t):
        rng = slice(8 * t, 8 * t + 8)
        here = plane(ref, field, p, rng)
        below, above = plane(ref, field, p - 1, rng), plane(ref, field, p + 1, rng)
        if t == 0:
            back = pltpu.roll(here, 1, 0)
        else:
            back = plane(ref, field, p, slice(8 * t - 1, 8 * t + 7))
        if t == tiles - 1:
            front = pltpu.roll(here, 7, 0)
        else:
            front = plane(ref, field, p, slice(8 * t + 1, 8 * t + 9))
        left = jnp.where(first, 0.0, pltpu.roll(here, 1, 1))
        right = jnp.where(last, 0.0, pltpu.roll(here, width - 1, 1))
        return (below + above) + (back + front) + (left + right)

    for p in range(planes + extra):
        for t in range(pad // 8, tiles - pad // 8):
            rng = slice(8 * t, 8 * t + 8)
            if p < planes:
                to_d, to_a = dn_ref.at[p, rng], an_ref.at[p, rng]
                bd, ba, gain, inv, own = (r[p, rng] for r in (bd_ref, ba_ref, gain_ref, inv_ref, own_ref))
            else:
                to_d, to_a = hn_ref.at[0, p - planes, rng], hn_ref.at[1, p - planes, rng]
                bd, ba, inv, gain, own = (deep_ref[i, p - planes, rng] for i in range(5))
                own = own.astype(jnp.int32)
            looked = jnp.concatenate(
                [_lookup(table, own[:, LANES * j : LANES * (j + 1)]) for j in range(width // LANES)],
                axis=1,
            )
            to_d[...] = (bd + near(d_ref, 0, p, t) + gain * looked) * inv
            acc = ba + near(a_ref, 1, p, t)
            if p == 0 and t == PAD // 8:
                acc = acc + source(block)
            if p == 0 and t == tiles - PAD // 8:
                acc = acc + source(block + 1)
            to_a[...] = acc * inv


def _ref_values(d_ref):
    width = d_ref.shape[2]
    lane = lax.broadcasted_iota(jnp.int32, (8, LANES), 1)
    row = d_ref[0, PAD : PAD + 8]
    got = jnp.zeros((8, LANES), jnp.float32)
    for j in range(width // LANES):
        part = jnp.broadcast_to(row[0:1, LANES * j : LANES * (j + 1)], (8, LANES))
        pick = jnp.take_along_axis(part, (lane & 3) * 32, axis=1, mode="promise_in_bounds")
        got = jnp.where((lane & 15) // 4 == j, pick, got)
    return lane, got


def _write_refs(scal_ref, d_ref, out_ref):
    core, block = scal_ref[0], scal_ref[1]
    lane, got = _ref_values(d_ref)
    for half in (0, 1):
        mine = (lane // 16 + 8 * half == block) & (core == 0)
        out_ref[:, half] = jnp.broadcast_to(
            jnp.where(mine, got, 0.0)[0:1], (out_ref.shape[0], LANES)
        )


def _collect(scal_ref, d_ref, a_ref, gain_ref, own_ref, hot_ref, out_ref, split_refs):
    planes, rows, width = d_ref.shape
    tiles = (rows - 2 * PAD) // 8
    _write_refs(scal_ref, d_ref, out_ref)
    for p in range(planes):
        for t in range(tiles):
            at = (p, slice(PAD + 8 * t, PAD + 8 * t + 8))
            y = gain_ref[at] * a_ref[at]
            coarse = y.astype(jnp.bfloat16).astype(jnp.float32)
            fine = y - coarse
            upper = own_ref[at] >= LANES
            base = (p * tiles + t) * 64
            terms = (
                jnp.where(upper, 0.0, coarse),
                jnp.where(upper, 0.0, fine),
                jnp.where(upper, coarse, 0.0),
                jnp.where(upper, fine, 0.0),
            )
            for j in range(width // LANES):
                for k, term in enumerate(terms):
                    split_refs[j][pl.ds(base + k, 8, stride=8), :] = term[:, LANES * j : LANES * (j + 1)]
    acc = jnp.zeros((8, LANES), jnp.float32)
    for line in range(hot_ref.shape[0]):
        vals = jnp.concatenate([ref[8 * line : 8 * line + 8, :] for ref in split_refs], axis=1)
        acc = acc + lax.dot_general(
            vals.astype(jnp.bfloat16), hot_ref[line], (((1,), (1,)), ((), ())),
            preferred_element_type=jnp.float32,
        )
    count = out_ref.shape[0]
    out_ref[:, 2] = jnp.broadcast_to(acc[0:1] + acc[1:2], (count, LANES))
    out_ref[:, 3] = jnp.broadcast_to(acc[2:3] + acc[3:4], (count, LANES))


def last_kernel(scal_ref, *refs):
    ins, (keep_ref, give_ref, out_ref, dn_ref, an_ref) = refs[:-5], refs[-5:]
    core, block = scal_ref[0], scal_ref[1]
    _sweep(scal_ref, *ins, dn_ref, an_ref, None, 0, PAD)
    planes, rows, width = dn_ref.shape
    radial = width // 2
    lane, values = _ref_values(dn_ref)
    line = jnp.where((lane // 16 == jnp.bitwise_and(block, 3)) & (core == 0), values, 0.0)[0:1]
    for i, ref in enumerate((dn_ref, an_ref)):
        acc = jnp.zeros((8, width), jnp.float32)
        for p in range(planes):
            for t in range((rows - 2 * PAD) // 8):
                v = ref[p, PAD + 8 * t : PAD + 8 * t + 8]
                acc = acc + v * v
                low, high = v[:, :radial], v[:, radial:]
                keep_ref[i, p, 8 * t : 8 * t + 8] = jnp.where(core == 0, low, high)
                give_ref[i, p, 8 * t : 8 * t + 8] = jnp.where(core == 0, high, low)
        acc = sum(acc[:, LANES * j : LANES * (j + 1)] for j in range(width // LANES))
        acc = acc + pltpu.roll(acc, 64, 1)
        acc = jnp.sum(acc + pltpu.roll(acc, 32, 1), axis=0, keepdims=True)
        line = jnp.where(lane[0:1] // 32 == 2 + i, acc, line)
    out_ref[...] = jnp.broadcast_to(line, out_ref.shape)


def fields_kernel(scal_ref, recv_ref, keep_ref, got_ref, gain_ref, own_ref, first_ref, second_ref,
                  *, cells, group):
    core, sector = scal_ref[0], scal_ref[2]
    planes, axial, radial = gain_ref.shape
    half = planes // 2
    lane = lax.broadcasted_iota(jnp.int32, (8, LANES), 1)
    quads = [
        jnp.broadcast_to(
            jnp.sum(recv_ref[pl.ds(pl.multiple_of(sector * group, 8) + 8 * j, 8), :], axis=0, keepdims=True),
            (8, LANES),
        )
        for j in range(4)
    ]
    table = [jnp.where(lane < 64, quads[2 * j], pltpu.roll(quads[2 * j + 1], 64, 1)) for j in (0, 1)]
    total = jnp.broadcast_to(jnp.sum(recv_ref[...], axis=0, keepdims=True), (8, LANES))
    squares = [
        jnp.sum(jnp.where(lane // 32 == 2 + i, total, 0.0), axis=1, keepdims=True)[0:1] / cells
        for i in (0, 1)
    ]
    scale = lax.rsqrt(squares[0] * squares[1] + 1e-12)
    for p in range(planes):
        for t in range(axial // 8):
            rng = slice(8 * t, 8 * t + 8)
            mine, at = (core == 0, p) if p < half else (core == 1, planes - 1 - p)
            direct, adjoint = (
                jnp.where(mine, keep_ref[i, at, rng], got_ref[i, at, rng]) for i in (0, 1)
            )
            own = own_ref[p, rng]
            looked = jnp.concatenate(
                [_lookup(table, own[:, LANES * j : LANES * (j + 1)]) for j in range(radial // LANES)],
                axis=1,
            )
            first_ref[p, rng] = adjoint * direct * scale
            second_ref[p, rng] = adjoint * (gain_ref[p, rng] * looked) * scale


def on_device(rhs_direct, rhs_adjoint, diag_shift, flame_gain, ref_owner):
    planes, axial, radial = rhs_direct.shape
    sectors, blocks = lax.axis_size("sector"), lax.axis_size("block")
    core, block = lax.axis_index("flame"), lax.axis_index("block")
    scal = jnp.stack([core, block, lax.axis_index("sector")]).astype(jnp.int32)
    half, width, rows = planes // 2, 2 * radial, axial + 2 * PAD
    swap = [(0, 1), (1, 0)]
    ring = [(2 * s, (2 * s - 1) % (2 * sectors)) for s in range(sectors)]
    ring += [(2 * s + 1, (2 * s + 2) % (2 * sectors)) for s in range(sectors)]

    def arr(*shape, dtype=jnp.float32):
        return jax.ShapeDtypeStruct(shape, dtype)

    quarter = arr(5, half, axial, radial)
    ids = pltpu.VMEM((half, axial, radial), jnp.int32)
    keep, give = _call(
        pack_kernel, (quarter, quarter), 5, [ids, ids, pltpu.SemaphoreType.DMA((5, half, 2))],
        name="pack", space=pltpu.HBM,
    )(scal, rhs_direct, rhs_adjoint, diag_shift, flame_gain, ref_owner)
    got = lax.ppermute(give, "flame", swap)
    edge = arr(5, half * HALO, width)
    first_rows, last_rows = _call(edges_kernel, (edge, edge), 2, name="edges")(scal, keep, got)
    before = lax.ppermute(last_rows, "block", [(i, i + 1) for i in range(blocks - 1)])
    after = lax.ppermute(first_rows, "block", [(i + 1, i) for i in range(blocks - 1)])

    field, plane = arr(half, rows, width), arr(2, rows, width)
    full = pltpu.VMEM((half, rows, width), jnp.float32)
    split = [pltpu.VMEM((half * axial * 8, LANES), jnp.float32)] * (width // LANES)
    message = arr(2 * blocks, 4, LANES)
    owners = arr(half, rows, width, dtype=jnp.int32)
    hot = _call(hot_kernel, arr(half * axial, LANES, width, dtype=jnp.bfloat16), 2, name="hot")(
        scal, keep, got
    )
    bd, ba, gain, inverse, owner, direct, adjoint, inner, outer, sent = _call(
        functools.partial(init_kernel, blocks=blocks),
        (field, field, field, field, owners, field, field, arr(5, INNER, rows, width), plane, message),
        5, [full, full] + split, name="init",
    )(scal, keep, got, before, after, hot)
    cut, layers = arr(2, half, axial, radial), (2, INNER, rows, width)
    everyone = 2 * blocks * sectors
    deep = halo = None
    for sweep in range(ITERS):
        outer_in = lax.ppermute(outer, ("sector", "flame"), ring)
        if sweep == 0:
            deep = lax.ppermute(inner, "flame", swap)
        elif sweep % INNER == 0:
            halo = lax.ppermute(halo, "flame", swap)
        recv = lax.all_to_all(sent, BF, 0, 0, tiled=True)
        args = (scal, recv, outer_in, direct, adjoint, bd, ba, gain, inverse, owner, deep)
        args += () if halo is None else (halo,)
        if sweep < ITERS - 1:
            step = functools.partial(
                step_kernel, extra=INNER - 1 - sweep % INNER, first=sweep == 0
            )
            scratch = ([pltpu.VMEM(layers, jnp.float32)] if sweep == 0 else []) + split
            direct, adjoint, halo, outer, sent = _call(
                step, (field, field, arr(*layers), plane, message), len(args), scratch, name="step"
            )(*args, hot)
        else:
            keep, give, sent = _call(
                last_kernel, (cut, cut, arr(everyone, LANES)), 11, [full, full], name="last"
            )(*args)

    got = lax.ppermute(give, "flame", swap)
    recv = lax.all_to_all(sent, ("sector",) + BF, 0, 0, tiled=True)
    out = arr(planes, axial, radial)
    cells = planes * axial * radial * everyone
    return tuple(
        _call(
            functools.partial(fields_kernel, cells=cells, group=2 * blocks), (out, out), 5, name="fields"
        )(scal, recv, keep, got, flame_gain, ref_owner)
    )


def solution(mesh):
    spec = P("sector", "block", "flame")
    return jax.shard_map(
        on_device,
        mesh=mesh,
        in_specs=(spec,) * 5,
        out_specs=(spec, spec),
        check_vma=False,
    )
```

```python
import functools

import jax
import jax.numpy as jnp
from jax import lax
from jax.experimental import pallas as pl
from jax.experimental.pallas import tpu as pltpu
from jax.sharding import PartitionSpec as P

ITERS = 6
REF_DEV = 8
GROUP = 16
INNER = 3
PAD = 8
HALO = 6
LANES = 128
INTERPRET = False
BF = ("block", "flame")


def _call(kernel, out_shape, n_in, scratch=(), name=None, space=pltpu.VMEM):
    vmem = pl.BlockSpec(memory_space=pltpu.VMEM)
    single = not isinstance(out_shape, (tuple, list))
    call = pl.pallas_call(
        kernel,
        out_shape=out_shape,
        in_specs=[pl.BlockSpec(memory_space=pltpu.SMEM)] + [pl.BlockSpec(memory_space=space)] * n_in,
        out_specs=vmem if single else [vmem] * len(out_shape),
        scratch_shapes=list(scratch),
        interpret=INTERPRET,
        name=name,
        compiler_params=pltpu.CompilerParams(vmem_limit_bytes=24 << 20),
    )
    if space is pltpu.VMEM or INTERPRET:
        return call
    return lambda scal, *args: call(
        scal, *(pltpu.with_memory_space_constraint(x, space) for x in args)
    )


def _lookup(table, owner):
    low = jnp.take_along_axis(table[0], owner & (LANES - 1), axis=1, mode="promise_in_bounds")
    high = jnp.take_along_axis(table[1], owner & (LANES - 1), axis=1, mode="promise_in_bounds")
    return jnp.where(owner < LANES, low, high)


def _table(total, row):
    return [jnp.broadcast_to(total[row + j : row + j + 1], (8, LANES)) for j in (0, 1)]


def pack_kernel(scal_ref, *refs):
    core = scal_ref[0]
    ins, (keep_ref, give_ref, keep_id, give_id, sems) = refs[:5], refs[5:]
    half = keep_ref.shape[1]
    copies = []
    for i, ref in enumerate(ins):
        for p in range(half):
            step = 2 * half - 1 - 2 * p
            for k, (dst, ids, at) in enumerate(
                ((keep_ref, keep_id, core), (give_ref, give_id, 1 - core))
            ):
                to = dst.at[i, p] if i < 4 else ids.at[p]
                copies.append(pltpu.make_async_copy(ref.at[p + at * step], to, sems.at[i, p, k]))
    for copy in copies:
        copy.start()
    for copy in copies:
        copy.wait()
    keep_ref[4] = keep_id[...].astype(jnp.float32)
    give_ref[4] = give_id[...].astype(jnp.float32)


def edges_kernel(scal_ref, keep_ref, got_ref, after_ref, before_ref):
    core = scal_ref[0]
    count, half, axial, radial = keep_ref.shape
    for i in range(count):
        for p in range(half):
            to = slice(p * HALO, (p + 1) * HALO)
            for ref, rng in ((after_ref, slice(0, HALO)), (before_ref, slice(axial - HALO, axial))):
                mine, other = keep_ref[i, p, rng], got_ref[i, p, rng]
                ref[i, to, :radial] = jnp.where(core == 0, mine, other)
                ref[i, to, radial:] = jnp.where(core == 0, other, mine)


def hot_kernel(scal_ref, keep_ref, got_ref, high_ref, low_ref, out_ref, d_ref, a_ref, gain_ref):
    core = scal_ref[0]
    count, half, axial, radial = keep_ref.shape
    width = 2 * radial
    ids = lax.broadcasted_iota(jnp.int32, (GROUP, width), 0).astype(jnp.float32)
    for p in range(half):
        for t in range(axial // 8):
            rng = slice(8 * t, 8 * t + 8)
            bd, ba, shift, gain, owner = (
                jnp.concatenate(
                    [jnp.where(core == h, keep_ref[i, p, rng], got_ref[i, p, rng]) for h in (0, 1)], axis=1
                )
                for i in range(count)
            )
            inv = 1.0 / (6.0 + shift)
            if p == 0:
                d_ref[0, rng] = bd * inv
            a_ref[p, rng] = ba * inv
            gain_ref[p, rng] = gain
            owner = owner.astype(jnp.int32)
            for part, ref in ((owner // GROUP, high_ref), (owner % GROUP, low_ref)):
                part = part.astype(jnp.float32)
                for x in range(8):
                    hit = jnp.broadcast_to(part[x : x + 1], (GROUP, width)) == ids
                    ref[(p * (axial // 8) + t) * 8 + x] = jnp.where(hit, 1.0, 0.0).astype(jnp.bfloat16)
    collect = _Collect(a_ref, gain_ref, high_ref, low_ref, 0)
    for p in range(half):
        collect.plane(p)
    collect.finish(out_ref)
    _write_refs(scal_ref, d_ref, out_ref, 0)


def init_kernel(scal_ref, keep_ref, got_ref, before_ref, after_ref, bd_ref, ba_ref, gain_ref,
                inv_ref, own_ref, d_ref, a_ref, inner_ref, outer_ref, shift_ref, id_ref, *, blocks):
    core, block = scal_ref[0], scal_ref[1]
    _, half, axial, radial = keep_ref.shape
    rows = axial + 2 * PAD
    for i, ref in enumerate((bd_ref, ba_ref, shift_ref, gain_ref, id_ref)):
        for p in range(half):
            ref[p, :PAD] = jnp.zeros((PAD, 2 * radial), jnp.float32)
            ref[p, rows - PAD :] = jnp.zeros((PAD, 2 * radial), jnp.float32)
            ref[p, PAD - HALO : PAD] = before_ref[i, p * HALO : (p + 1) * HALO]
            ref[p, rows - PAD : rows - PAD + HALO] = after_ref[i, p * HALO : (p + 1) * HALO]
            mine, other = keep_ref[i, p], got_ref[i, p]
            ref[p, PAD : PAD + axial, :radial] = jnp.where(core == 0, mine, other)
            ref[p, PAD : PAD + axial, radial:] = jnp.where(core == 0, other, mine)
    for p in range(half):
        for t in range(rows // 8):
            at = (p, slice(8 * t, 8 * t + 8))
            inv = 1.0 / (6.0 + shift_ref[at])
            if t < PAD // 8:
                inv = jnp.where(block == 0, 0.0, inv)
            if t >= (rows - PAD) // 8:
                inv = jnp.where(block == blocks - 1, 0.0, inv)
            inv_ref[at] = inv
            own_ref[at] = id_ref[at].astype(jnp.int32)
            d_ref[at] = bd_ref[at] * inv
            a_ref[at] = ba_ref[at] * inv
    for i, ref in enumerate((bd_ref, ba_ref, inv_ref, gain_ref, id_ref)):
        for depth in range(INNER):
            inner_ref[i, depth] = ref[half - 1 - depth]
    _send(outer_ref, d_ref, a_ref)


def _send(outer_ref, d_ref, a_ref):
    outer_ref[0] = d_ref[0]
    outer_ref[1] = a_ref[0]


def step_kernel(scal_ref, *refs, extra, first):
    refs = list(refs)
    ins = [refs.pop(0) for _ in range(10)]
    halo_ref = None if first else refs.pop(0)
    high_ref, low_ref = refs.pop(0), refs.pop(0)
    dn_ref, an_ref, hn_ref, outer_ref, out_ref = [refs.pop(0) for _ in range(5)]
    if first:
        halo_ref = refs.pop(0)
        for i in (0, 1):
            for depth in range(INNER):
                halo_ref[i, depth] = ins[9][i, depth] * ins[9][2, depth]
    collect = _Collect(an_ref, ins[6], high_ref, low_ref, PAD)
    _sweep(scal_ref, *ins, halo_ref, dn_ref, an_ref, hn_ref, extra, 0, collect)
    if not extra:
        for i, ref in enumerate((dn_ref, an_ref)):
            for depth in range(INNER):
                hn_ref[i, depth] = ref[ref.shape[0] - 1 - depth]
    _send(outer_ref, dn_ref, an_ref)
    collect.finish(out_ref)
    _write_refs(scal_ref, dn_ref, out_ref, PAD)


def _sweep(scal_ref, recv_ref, outer_ref, d_ref, a_ref, bd_ref, ba_ref, gain_ref,
           inv_ref, own_ref, deep_ref, halo_ref, dn_ref, an_ref, hn_ref, extra, pad=0, collect=None):
    core, block = scal_ref[0], scal_ref[1]
    planes, rows, width = d_ref.shape
    tiles = rows // 8
    total = jnp.sum(recv_ref[...], axis=0)
    table = _table(total, 0)
    sums = _table(total, 2)
    lane = lax.broadcasted_iota(jnp.int32, (8, LANES), 1)
    sub = lax.broadcasted_iota(jnp.int32, (8, LANES), 0)
    spot = (lane % 32 == 0) & (sub == 0) & (core == 0)
    first = lax.broadcasted_iota(jnp.int32, (8, width), 1) == 0
    last = lax.broadcasted_iota(jnp.int32, (8, width), 1) == width - 1

    def source(blk):
        tab = jnp.where(blk < 8, sums[0], sums[1])
        parts = []
        for j in range(width // LANES):
            at = jnp.bitwise_and(blk, 7) * 16 + 4 * j + lane // 32
            got = jnp.take_along_axis(tab, at & (LANES - 1), axis=1, mode="promise_in_bounds")
            parts.append(jnp.where(spot, got, 0.0))
        return jnp.concatenate(parts, axis=1)

    def plane(ref, field, p, rng):
        if p < 0:
            return outer_ref[field, rng]
        return ref[p, rng] if p < planes else halo_ref[field, p - planes, rng]

    def near(ref, field, p, t):
        rng = slice(8 * t, 8 * t + 8)
        here = plane(ref, field, p, rng)
        below, above = plane(ref, field, p - 1, rng), plane(ref, field, p + 1, rng)
        if t == 0:
            back = pltpu.roll(here, 1, 0)
        else:
            back = plane(ref, field, p, slice(8 * t - 1, 8 * t + 7))
        if t == tiles - 1:
            front = pltpu.roll(here, 7, 0)
        else:
            front = plane(ref, field, p, slice(8 * t + 1, 8 * t + 9))
        left = jnp.where(first, 0.0, pltpu.roll(here, 1, 1))
        right = jnp.where(last, 0.0, pltpu.roll(here, width - 1, 1))
        return (below + above) + (back + front) + (left + right)

    for p in range(planes + extra):
        for t in range(pad // 8, tiles - pad // 8):
            rng = slice(8 * t, 8 * t + 8)
            if p < planes:
                to_d, to_a = dn_ref.at[p, rng], an_ref.at[p, rng]
                bd, ba, gain, inv, own = (r[p, rng] for r in (bd_ref, ba_ref, gain_ref, inv_ref, own_ref))
            else:
                to_d, to_a = hn_ref.at[0, p - planes, rng], hn_ref.at[1, p - planes, rng]
                bd, ba, inv, gain, own = (deep_ref[i, p - planes, rng] for i in range(5))
                own = own.astype(jnp.int32)
            looked = jnp.concatenate(
                [_lookup(table, own[:, LANES * j : LANES * (j + 1)]) for j in range(width // LANES)],
                axis=1,
            )
            to_d[...] = (bd + near(d_ref, 0, p, t) + gain * looked) * inv
            acc = ba + near(a_ref, 1, p, t)
            if p == 0 and t == PAD // 8:
                acc = acc + source(block)
            if p == 0 and t == tiles - PAD // 8:
                acc = acc + source(block + 1)
            to_a[...] = acc * inv
            if collect is not None:
                collect.some()
        if collect is not None and p < planes:
            collect.plane(p)


def _ref_values(d_ref, pad=PAD):
    width = d_ref.shape[2]
    lane = lax.broadcasted_iota(jnp.int32, (8, LANES), 1)
    row = d_ref[0, pad : pad + 8]
    got = jnp.zeros((8, LANES), jnp.float32)
    for j in range(width // LANES):
        part = jnp.broadcast_to(row[0:1, LANES * j : LANES * (j + 1)], (8, LANES))
        pick = jnp.take_along_axis(part, (lane & 3) * 32, axis=1, mode="promise_in_bounds")
        got = jnp.where((lane & 15) // 4 == j, pick, got)
    return lane, got


def _write_refs(scal_ref, d_ref, out_ref, pad):
    core, block = scal_ref[0], scal_ref[1]
    lane, got = _ref_values(d_ref, pad)
    for half in (0, 1):
        mine = (lane // 16 + 8 * half == block) & (core == 0)
        out_ref[:, half] = jnp.broadcast_to(
            jnp.where(mine, got, 0.0)[0:1], (out_ref.shape[0], LANES)
        )


class _Collect:

    def __init__(self, a_ref, gain_ref, high_ref, low_ref, pad):
        self.refs, self.hot, self.pad = (a_ref, gain_ref), (high_ref, low_ref), pad
        self.todo = []
        self.acc = jnp.zeros((2 * GROUP, GROUP), jnp.float32)

    def plane(self, p):
        a_ref, gain_ref = self.refs
        tiles = (a_ref.shape[1] - 2 * self.pad) // 8
        for t in range(tiles):
            at = (p, slice(self.pad + 8 * t, self.pad + 8 * t + 8))
            y = gain_ref[at] * a_ref[at]
            coarse = y.astype(jnp.bfloat16).astype(jnp.float32)
            self.todo += [((p * tiles + t) * 8 + x, x, coarse, y - coarse) for x in range(8)]

    def some(self, count=4):
        now, self.todo = self.todo[:count], self.todo[count:]
        for line, x, coarse, fine in now:
            high = self.hot[0][line]
            vals = jnp.concatenate(
                [
                    high * jnp.broadcast_to(v[x : x + 1], high.shape).astype(jnp.bfloat16)
                    for v in (coarse, fine)
                ],
                axis=0,
            )
            self.acc = self.acc + lax.dot_general(
                vals, self.hot[1][line], (((1,), (1,)), ((), ())), preferred_element_type=jnp.float32
            )

    def finish(self, out_ref):
        self.some(len(self.todo))
        both = self.acc[:GROUP] + self.acc[GROUP:]
        both = jnp.concatenate([both, jnp.zeros((GROUP, LANES - GROUP), jnp.float32)], axis=1)
        sub = lax.broadcasted_iota(jnp.int32, (8, LANES), 0)
        for h in (0, 1):
            part = both[8 * h : 8 * h + 8]
            flat = part
            for i in range(1, 8):
                flat = jnp.where(sub == i, pltpu.roll(part, GROUP * i, 1), flat)
            out_ref[:, 2 + h] = jnp.broadcast_to(
                jnp.sum(flat, axis=0, keepdims=True), (out_ref.shape[0], LANES)
            )


def last_kernel(scal_ref, *refs):
    ins, (keep_ref, give_ref, out_ref, dn_ref, an_ref) = refs[:-5], refs[-5:]
    core, block = scal_ref[0], scal_ref[1]
    _sweep(scal_ref, *ins, dn_ref, an_ref, None, 0, PAD)
    planes, rows, width = dn_ref.shape
    radial = width // 2
    lane, values = _ref_values(dn_ref)
    line = jnp.where((lane // 16 == jnp.bitwise_and(block, 3)) & (core == 0), values, 0.0)[0:1]
    for i, ref in enumerate((dn_ref, an_ref)):
        acc = jnp.zeros((8, width), jnp.float32)
        for p in range(planes):
            for t in range((rows - 2 * PAD) // 8):
                v = ref[p, PAD + 8 * t : PAD + 8 * t + 8]
                acc = acc + v * v
                low, high = v[:, :radial], v[:, radial:]
                keep_ref[i, p, 8 * t : 8 * t + 8] = jnp.where(core == 0, low, high)
                give_ref[i, p, 8 * t : 8 * t + 8] = jnp.where(core == 0, high, low)
        acc = sum(acc[:, LANES * j : LANES * (j + 1)] for j in range(width // LANES))
        acc = acc + pltpu.roll(acc, 64, 1)
        acc = jnp.sum(acc + pltpu.roll(acc, 32, 1), axis=0, keepdims=True)
        line = jnp.where(lane[0:1] // 32 == 2 + i, acc, line)
    out_ref[...] = jnp.broadcast_to(line, out_ref.shape)


def fields_kernel(scal_ref, recv_ref, keep_ref, got_ref, gain_ref, own_ref, first_ref, second_ref,
                  *, cells, group):
    core, sector = scal_ref[0], scal_ref[2]
    planes, axial, radial = gain_ref.shape
    half = planes // 2
    lane = lax.broadcasted_iota(jnp.int32, (8, LANES), 1)
    quads = [
        jnp.broadcast_to(
            jnp.sum(recv_ref[pl.ds(pl.multiple_of(sector * group, 8) + 8 * j, 8), :], axis=0, keepdims=True),
            (8, LANES),
        )
        for j in range(4)
    ]
    table = [jnp.where(lane < 64, quads[2 * j], pltpu.roll(quads[2 * j + 1], 64, 1)) for j in (0, 1)]
    total = jnp.broadcast_to(jnp.sum(recv_ref[...], axis=0, keepdims=True), (8, LANES))
    squares = [
        jnp.sum(jnp.where(lane // 32 == 2 + i, total, 0.0), axis=1, keepdims=True)[0:1] / cells
        for i in (0, 1)
    ]
    scale = lax.rsqrt(squares[0] * squares[1] + 1e-12)
    for p in range(planes):
        for t in range(axial // 8):
            rng = slice(8 * t, 8 * t + 8)
            mine, at = (core == 0, p) if p < half else (core == 1, planes - 1 - p)
            direct, adjoint = (
                jnp.where(mine, keep_ref[i, at, rng], got_ref[i, at, rng]) for i in (0, 1)
            )
            own = own_ref[p, rng]
            looked = jnp.concatenate(
                [_lookup(table, own[:, LANES * j : LANES * (j + 1)]) for j in range(radial // LANES)],
                axis=1,
            )
            first_ref[p, rng] = adjoint * direct * scale
            second_ref[p, rng] = adjoint * (gain_ref[p, rng] * looked) * scale


def on_device(rhs_direct, rhs_adjoint, diag_shift, flame_gain, ref_owner):
    planes, axial, radial = rhs_direct.shape
    sectors, blocks = lax.axis_size("sector"), lax.axis_size("block")
    core, block = lax.axis_index("flame"), lax.axis_index("block")
    scal = jnp.stack([core, block, lax.axis_index("sector")]).astype(jnp.int32)
    half, width, rows = planes // 2, 2 * radial, axial + 2 * PAD
    swap = [(0, 1), (1, 0)]
    ring = [(2 * s, (2 * s - 1) % (2 * sectors)) for s in range(sectors)]
    ring += [(2 * s + 1, (2 * s + 2) % (2 * sectors)) for s in range(sectors)]

    def arr(*shape, dtype=jnp.float32):
        return jax.ShapeDtypeStruct(shape, dtype)

    quarter = arr(5, half, axial, radial)
    ids = pltpu.VMEM((half, axial, radial), jnp.int32)
    keep, give = _call(
        pack_kernel, (quarter, quarter), 5, [ids, ids, pltpu.SemaphoreType.DMA((5, half, 2))],
        name="pack", space=pltpu.HBM,
    )(scal, rhs_direct, rhs_adjoint, diag_shift, flame_gain, ref_owner)
    got = lax.ppermute(give, "flame", swap)
    edge = arr(5, half * HALO, width)
    first_rows, last_rows = _call(edges_kernel, (edge, edge), 2, name="edges")(scal, keep, got)
    before = lax.ppermute(last_rows, "block", [(i, i + 1) for i in range(blocks - 1)])
    after = lax.ppermute(first_rows, "block", [(i + 1, i) for i in range(blocks - 1)])

    field, plane = arr(half, rows, width), arr(2, rows, width)
    full = pltpu.VMEM((half, rows, width), jnp.float32)
    message = arr(2 * blocks, 4, LANES)
    owners = arr(half, rows, width, dtype=jnp.int32)
    own_cells = pltpu.VMEM((half, axial, width), jnp.float32)
    hot = arr(half * axial, GROUP, width, dtype=jnp.bfloat16)
    high, low, sent = _call(
        hot_kernel, (hot, hot, message), 2,
        [pltpu.VMEM((1, axial, width), jnp.float32), own_cells, own_cells], name="hot",
    )(scal, keep, got)
    bd, ba, gain, inverse, owner, direct, adjoint, inner, outer = _call(
        functools.partial(init_kernel, blocks=blocks),
        (field, field, field, field, owners, field, field, arr(5, INNER, rows, width), plane),
        4, [full, full], name="init",
    )(scal, keep, got, before, after)
    sent, outer, inner = lax.optimization_barrier((sent, outer, inner))
    cut, layers = arr(2, half, axial, radial), (2, INNER, rows, width)
    everyone = 2 * blocks * sectors
    deep = halo = None
    for sweep in range(ITERS):
        outer_in = lax.ppermute(outer, ("sector", "flame"), ring)
        if sweep == 0:
            deep = lax.ppermute(inner, "flame", swap)
        elif sweep % INNER == 0:
            halo = lax.ppermute(halo, "flame", swap)
        recv = lax.all_to_all(sent, BF, 0, 0, tiled=True)
        args = (scal, recv, outer_in, direct, adjoint, bd, ba, gain, inverse, owner, deep)
        args += () if halo is None else (halo,)
        if sweep < ITERS - 1:
            step = functools.partial(
                step_kernel, extra=INNER - 1 - sweep % INNER, first=sweep == 0
            )
            scratch = [pltpu.VMEM(layers, jnp.float32)] if sweep == 0 else []
            direct, adjoint, halo, outer, sent = _call(
                step, (field, field, arr(*layers), plane, message), len(args) + 1, scratch, name="step"
            )(*args, high, low)
        else:
            keep, give, sent = _call(
                last_kernel, (cut, cut, arr(everyone, LANES)), 11, [full, full], name="last"
            )(*args)

    got = lax.ppermute(give, "flame", swap)
    recv = lax.all_to_all(sent, ("sector",) + BF, 0, 0, tiled=True)
    out = arr(planes, axial, radial)
    cells = planes * axial * radial * everyone
    return tuple(
        _call(
            functools.partial(fields_kernel, cells=cells, group=2 * blocks), (out, out), 5, name="fields"
        )(scal, recv, keep, got, flame_gain, ref_owner)
    )


def solution(mesh):
    spec = P("sector", "block", "flame")
    return jax.shard_map(
        on_device,
        mesh=mesh,
        in_specs=(spec,) * 5,
        out_specs=(spec, spec),
        check_vma=False,
    )
```

```python
import functools

import jax
import jax.numpy as jnp
from jax import lax
from jax.experimental import pallas as pl
from jax.experimental.pallas import tpu as pltpu
from jax.sharding import PartitionSpec as P

ITERS = 6
REF_DEV = 8
GROUP = 16
INNER = 3
PAD = 8
HALO = 6
LANES = 128
INTERPRET = False
BF = ("block", "flame")


def _call(kernel, out_shape, n_in, scratch=(), name=None, space=pltpu.VMEM):
    vmem = pl.BlockSpec(memory_space=pltpu.VMEM)
    single = not isinstance(out_shape, (tuple, list))

    def body(*refs):
        kernel([lax.axis_index(axis) for axis in ("flame", "block", "sector")], *refs)

    call = pl.pallas_call(
        body,
        out_shape=out_shape,
        in_specs=[pl.BlockSpec(memory_space=space)] * n_in,
        out_specs=vmem if single else [vmem] * len(out_shape),
        scratch_shapes=list(scratch),
        interpret=INTERPRET,
        name=name,
        compiler_params=pltpu.CompilerParams(vmem_limit_bytes=24 << 20),
    )
    if space is pltpu.VMEM or INTERPRET:
        return call
    return lambda *args: call(*(pltpu.with_memory_space_constraint(x, space) for x in args))


def _lookup(table, owner):
    low = jnp.take_along_axis(table[0], owner & (LANES - 1), axis=1, mode="promise_in_bounds")
    high = jnp.take_along_axis(table[1], owner & (LANES - 1), axis=1, mode="promise_in_bounds")
    return jnp.where(owner < LANES, low, high)


def _table(total, row):
    return [jnp.broadcast_to(total[row + j : row + j + 1], (8, LANES)) for j in (0, 1)]


def pack_kernel(here, *refs):
    core = here[0]
    ins, (keep_ref, give_ref, keep_id, give_id, sems) = refs[:5], refs[5:]
    half = keep_ref.shape[1]
    copies = []
    for i, ref in enumerate(ins):
        for p in range(half):
            step = 2 * half - 1 - 2 * p
            for k, (dst, ids, at) in enumerate(
                ((keep_ref, keep_id, core), (give_ref, give_id, 1 - core))
            ):
                to = dst.at[i, p] if i < 4 else ids.at[p]
                copies.append(pltpu.make_async_copy(ref.at[p + at * step], to, sems.at[i, p, k]))
    for copy in copies:
        copy.start()
    for copy in copies:
        copy.wait()
    keep_ref[4] = keep_id[...].astype(jnp.float32)
    give_ref[4] = give_id[...].astype(jnp.float32)


def edges_kernel(here, keep_ref, got_ref, after_ref, before_ref):
    core = here[0]
    count, half, axial, radial = keep_ref.shape
    for i in range(count):
        for p in range(half):
            to = slice(p * HALO, (p + 1) * HALO)
            for ref, rng in ((after_ref, slice(0, HALO)), (before_ref, slice(axial - HALO, axial))):
                mine, other = keep_ref[i, p, rng], got_ref[i, p, rng]
                ref[i, to, :radial] = jnp.where(core == 0, mine, other)
                ref[i, to, radial:] = jnp.where(core == 0, other, mine)


def hot_kernel(here, keep_ref, got_ref, high_ref, low_ref, out_ref, d_ref, a_ref, gain_ref):
    core = here[0]
    count, half, axial, radial = keep_ref.shape
    width = 2 * radial
    ids = lax.broadcasted_iota(jnp.int32, (GROUP, width), 0).astype(jnp.float32)
    for p in range(half):
        for t in range(axial // 8):
            rng = slice(8 * t, 8 * t + 8)
            bd, ba, shift, gain, owner = (
                jnp.concatenate(
                    [jnp.where(core == h, keep_ref[i, p, rng], got_ref[i, p, rng]) for h in (0, 1)], axis=1
                )
                for i in range(count)
            )
            inv = 1.0 / (6.0 + shift)
            if p == 0:
                d_ref[0, rng] = bd * inv
            a_ref[p, rng] = ba * inv
            gain_ref[p, rng] = gain
            owner = owner.astype(jnp.int32)
            for part, ref in ((owner // GROUP, high_ref), (owner % GROUP, low_ref)):
                part = part.astype(jnp.float32)
                for x in range(8):
                    hit = jnp.broadcast_to(part[x : x + 1], (GROUP, width)) == ids
                    ref[(p * (axial // 8) + t) * 8 + x] = jnp.where(hit, 1.0, 0.0).astype(jnp.bfloat16)
    collect = _Collect(gain_ref, high_ref, low_ref, 0)
    for p in range(half):
        for t in range(axial // 8):
            collect.tile(p, t, a_ref[p, 8 * t : 8 * t + 8])
    collect.finish(out_ref)
    _write_refs(here, d_ref, out_ref, 0)


def init_kernel(here, keep_ref, got_ref, before_ref, after_ref, bd_ref, ba_ref, gain_ref,
                inv_ref, own_ref, d_ref, a_ref, inner_ref, outer_ref, shift_ref, id_ref, *, blocks):
    core, block = here[0], here[1]
    _, half, axial, radial = keep_ref.shape
    rows = axial + 2 * PAD
    for i, ref in enumerate((bd_ref, ba_ref, shift_ref, gain_ref, id_ref)):
        for p in range(half):
            ref[p, :PAD] = jnp.zeros((PAD, 2 * radial), jnp.float32)
            ref[p, rows - PAD :] = jnp.zeros((PAD, 2 * radial), jnp.float32)
            ref[p, PAD - HALO : PAD] = before_ref[i, p * HALO : (p + 1) * HALO]
            ref[p, rows - PAD : rows - PAD + HALO] = after_ref[i, p * HALO : (p + 1) * HALO]
            mine, other = keep_ref[i, p], got_ref[i, p]
            ref[p, PAD : PAD + axial, :radial] = jnp.where(core == 0, mine, other)
            ref[p, PAD : PAD + axial, radial:] = jnp.where(core == 0, other, mine)
    for p in range(half):
        for t in range(rows // 8):
            at = (p, slice(8 * t, 8 * t + 8))
            inv = 1.0 / (6.0 + shift_ref[at])
            if t < PAD // 8:
                inv = jnp.where(block == 0, 0.0, inv)
            if t >= (rows - PAD) // 8:
                inv = jnp.where(block == blocks - 1, 0.0, inv)
            inv_ref[at] = inv
            own_ref[at] = id_ref[at].astype(jnp.int32)
            d_ref[at] = bd_ref[at] * inv
            a_ref[at] = ba_ref[at] * inv
    for i, ref in enumerate((bd_ref, ba_ref, inv_ref, gain_ref, id_ref)):
        for depth in range(INNER):
            inner_ref[i, depth] = ref[half - 1 - depth]
    _send(outer_ref, d_ref, a_ref)


def _send(outer_ref, d_ref, a_ref):
    outer_ref[0] = d_ref[0]
    outer_ref[1] = a_ref[0]


def step_kernel(here, *refs, extra, first):
    refs = list(refs)
    ins = [refs.pop(0) for _ in range(10)]
    halo_ref = None if first else refs.pop(0)
    high_ref, low_ref = refs.pop(0), refs.pop(0)
    dn_ref, an_ref, hn_ref, outer_ref, out_ref = [refs.pop(0) for _ in range(5)]
    if first:
        halo_ref = refs.pop(0)
        for i in (0, 1):
            for depth in range(INNER):
                halo_ref[i, depth] = ins[9][i, depth] * ins[9][2, depth]
    collect = _Collect(ins[6], high_ref, low_ref, PAD)
    _sweep(here, *ins, halo_ref, dn_ref, an_ref, hn_ref, extra, 0, collect)
    if not extra:
        for i, ref in enumerate((dn_ref, an_ref)):
            for depth in range(INNER):
                hn_ref[i, depth] = ref[ref.shape[0] - 1 - depth]
    _send(outer_ref, dn_ref, an_ref)
    collect.finish(out_ref)
    _write_refs(here, dn_ref, out_ref, PAD)


def _sweep(here, recv_ref, outer_ref, d_ref, a_ref, bd_ref, ba_ref, gain_ref,
           inv_ref, own_ref, deep_ref, halo_ref, dn_ref, an_ref, hn_ref, extra, pad=0, collect=None):
    core, block = here[0], here[1]
    planes, rows, width = d_ref.shape
    tiles = rows // 8
    total = jnp.sum(recv_ref[...], axis=0)
    table = _table(total, 0)
    sums = _table(total, 2)
    lane = lax.broadcasted_iota(jnp.int32, (8, LANES), 1)
    sub = lax.broadcasted_iota(jnp.int32, (8, LANES), 0)
    spot = (lane % 32 == 0) & (sub == 0) & (core == 0)
    first = lax.broadcasted_iota(jnp.int32, (8, width), 1) == 0
    last = lax.broadcasted_iota(jnp.int32, (8, width), 1) == width - 1

    def source(blk):
        tab = jnp.where(blk < 8, sums[0], sums[1])
        parts = []
        for j in range(width // LANES):
            at = jnp.bitwise_and(blk, 7) * 16 + 4 * j + lane // 32
            got = jnp.take_along_axis(tab, at & (LANES - 1), axis=1, mode="promise_in_bounds")
            parts.append(jnp.where(spot, got, 0.0))
        return jnp.concatenate(parts, axis=1)

    def plane(ref, field, p, rng):
        if p < 0:
            return outer_ref[field, rng]
        return ref[p, rng] if p < planes else halo_ref[field, p - planes, rng]

    def near(ref, field, p, t, below, mid, above):
        if t == 0:
            back = pltpu.roll(mid, 1, 0)
        else:
            back = plane(ref, field, p, slice(8 * t - 1, 8 * t + 7))
        if t == tiles - 1:
            front = pltpu.roll(mid, 7, 0)
        else:
            front = plane(ref, field, p, slice(8 * t + 1, 8 * t + 9))
        left = jnp.where(first, 0.0, pltpu.roll(mid, 1, 1))
        right = jnp.where(last, 0.0, pltpu.roll(mid, width - 1, 1))
        return (below + above) + (back + front) + (left + right)

    own_tiles = range(PAD // 8, tiles - PAD // 8)
    rest = [t for t in range(tiles) if t not in own_tiles] if pad == 0 else []
    for t in list(own_tiles) + rest:
        rng = slice(8 * t, 8 * t + 8)
        window = [[plane(r, i, p, rng) for p in (-1, 0)] for i, r in enumerate((d_ref, a_ref))]
        for p in range(planes + extra):
            if p < planes:
                to_d, to_a = dn_ref.at[p, rng], an_ref.at[p, rng]
                bd, ba, gain, inv, own = (r[p, rng] for r in (bd_ref, ba_ref, gain_ref, inv_ref, own_ref))
            else:
                to_d, to_a = hn_ref.at[0, p - planes, rng], hn_ref.at[1, p - planes, rng]
                bd, ba, inv, gain, own = (deep_ref[i, p - planes, rng] for i in range(5))
                own = own.astype(jnp.int32)
            for i, r in enumerate((d_ref, a_ref)):
                window[i] = window[i][-2:] + [plane(r, i, p + 1, rng)]
            looked = jnp.concatenate(
                [_lookup(table, own[:, LANES * j : LANES * (j + 1)]) for j in range(width // LANES)],
                axis=1,
            )
            to_d[...] = (bd + near(d_ref, 0, p, t, *window[0]) + gain * looked) * inv
            acc = ba + near(a_ref, 1, p, t, *window[1])
            if p == 0 and t == PAD // 8:
                acc = acc + source(block)
            if p == 0 and t == tiles - PAD // 8:
                acc = acc + source(block + 1)
            acc = acc * inv
            to_a[...] = acc
            if collect is not None:
                collect.some()
                if p < planes and t in own_tiles:
                    collect.tile(p, t - PAD // 8, acc)


def _ref_values(d_ref, pad=PAD):
    width = d_ref.shape[2]
    lane = lax.broadcasted_iota(jnp.int32, (8, LANES), 1)
    row = d_ref[0, pad : pad + 8]
    got = jnp.zeros((8, LANES), jnp.float32)
    for j in range(width // LANES):
        part = jnp.broadcast_to(row[0:1, LANES * j : LANES * (j + 1)], (8, LANES))
        pick = jnp.take_along_axis(part, (lane & 3) * 32, axis=1, mode="promise_in_bounds")
        got = jnp.where((lane & 15) // 4 == j, pick, got)
    return lane, got


def _write_refs(here, d_ref, out_ref, pad):
    core, block = here[0], here[1]
    lane, got = _ref_values(d_ref, pad)
    for half in (0, 1):
        mine = (lane // 16 + 8 * half == block) & (core == 0)
        out_ref[:, half] = jnp.broadcast_to(
            jnp.where(mine, got, 0.0)[0:1], (out_ref.shape[0], LANES)
        )


class _Collect:

    def __init__(self, gain_ref, high_ref, low_ref, pad):
        self.gain, self.hot, self.pad = gain_ref, (high_ref, low_ref), pad
        self.todo = []
        self.acc = jnp.zeros((2 * GROUP, GROUP), jnp.float32)

    def tile(self, p, t, a):
        gain_ref, tiles = self.gain, (self.gain.shape[1] - 2 * self.pad) // 8
        y = gain_ref[p, self.pad + 8 * t : self.pad + 8 * t + 8] * a
        coarse = y.astype(jnp.bfloat16).astype(jnp.float32)
        self.todo += [((p * tiles + t) * 8 + x, x, coarse, y - coarse) for x in range(8)]

    def some(self, count=4):
        now, self.todo = self.todo[:count], self.todo[count:]
        for line, x, coarse, fine in now:
            high = self.hot[0][line]
            vals = jnp.concatenate(
                [
                    high * jnp.broadcast_to(v[x : x + 1], high.shape).astype(jnp.bfloat16)
                    for v in (coarse, fine)
                ],
                axis=0,
            )
            self.acc = self.acc + lax.dot_general(
                vals, self.hot[1][line], (((1,), (1,)), ((), ())), preferred_element_type=jnp.float32
            )

    def finish(self, out_ref):
        self.some(len(self.todo))
        both = self.acc[:GROUP] + self.acc[GROUP:]
        both = jnp.concatenate([both, jnp.zeros((GROUP, LANES - GROUP), jnp.float32)], axis=1)
        sub = lax.broadcasted_iota(jnp.int32, (8, LANES), 0)
        for h in (0, 1):
            part = both[8 * h : 8 * h + 8]
            flat = part
            for i in range(1, 8):
                flat = jnp.where(sub == i, pltpu.roll(part, GROUP * i, 1), flat)
            out_ref[:, 2 + h] = jnp.broadcast_to(
                jnp.sum(flat, axis=0, keepdims=True), (out_ref.shape[0], LANES)
            )


def last_kernel(here, *refs):
    ins, (keep_ref, give_ref, out_ref, dn_ref, an_ref) = refs[:-5], refs[-5:]
    core, block = here[0], here[1]
    _sweep(here, *ins, dn_ref, an_ref, None, 0, PAD)
    planes, rows, width = dn_ref.shape
    radial = width // 2
    lane, values = _ref_values(dn_ref)
    line = jnp.where((lane // 16 == jnp.bitwise_and(block, 3)) & (core == 0), values, 0.0)[0:1]
    for i, ref in enumerate((dn_ref, an_ref)):
        acc = jnp.zeros((8, width), jnp.float32)
        for p in range(planes):
            for t in range((rows - 2 * PAD) // 8):
                v = ref[p, PAD + 8 * t : PAD + 8 * t + 8]
                acc = acc + v * v
                low, high = v[:, :radial], v[:, radial:]
                keep_ref[i, p, 8 * t : 8 * t + 8] = jnp.where(core == 0, low, high)
                give_ref[i, p, 8 * t : 8 * t + 8] = jnp.where(core == 0, high, low)
        acc = sum(acc[:, LANES * j : LANES * (j + 1)] for j in range(width // LANES))
        acc = acc + pltpu.roll(acc, 64, 1)
        acc = jnp.sum(acc + pltpu.roll(acc, 32, 1), axis=0, keepdims=True)
        line = jnp.where(lane[0:1] // 32 == 2 + i, acc, line)
    out_ref[...] = jnp.broadcast_to(line, out_ref.shape)


def fields_kernel(here, recv_ref, keep_ref, got_ref, gain_ref, own_ref, first_ref, second_ref,
                  *, cells, group):
    core, sector = here[0], here[2]
    planes, axial, radial = gain_ref.shape
    half = planes // 2
    lane = lax.broadcasted_iota(jnp.int32, (8, LANES), 1)
    quads = [
        jnp.broadcast_to(
            jnp.sum(recv_ref[pl.ds(pl.multiple_of(sector * group, 8) + 8 * j, 8), :], axis=0, keepdims=True),
            (8, LANES),
        )
        for j in range(4)
    ]
    table = [jnp.where(lane < 64, quads[2 * j], pltpu.roll(quads[2 * j + 1], 64, 1)) for j in (0, 1)]
    total = jnp.broadcast_to(jnp.sum(recv_ref[...], axis=0, keepdims=True), (8, LANES))
    squares = [
        jnp.sum(jnp.where(lane // 32 == 2 + i, total, 0.0), axis=1, keepdims=True)[0:1] / cells
        for i in (0, 1)
    ]
    scale = lax.rsqrt(squares[0] * squares[1] + 1e-12)
    for p in range(planes):
        for t in range(axial // 8):
            rng = slice(8 * t, 8 * t + 8)
            mine, at = (core == 0, p) if p < half else (core == 1, planes - 1 - p)
            direct, adjoint = (
                jnp.where(mine, keep_ref[i, at, rng], got_ref[i, at, rng]) for i in (0, 1)
            )
            own = own_ref[p, rng]
            looked = jnp.concatenate(
                [_lookup(table, own[:, LANES * j : LANES * (j + 1)]) for j in range(radial // LANES)],
                axis=1,
            )
            first_ref[p, rng] = adjoint * direct * scale
            second_ref[p, rng] = adjoint * (gain_ref[p, rng] * looked) * scale


def on_device(rhs_direct, rhs_adjoint, diag_shift, flame_gain, ref_owner):
    planes, axial, radial = rhs_direct.shape
    sectors, blocks = lax.axis_size("sector"), lax.axis_size("block")
    half, width, rows = planes // 2, 2 * radial, axial + 2 * PAD
    swap = [(0, 1), (1, 0)]
    ring = [(2 * s, (2 * s - 1) % (2 * sectors)) for s in range(sectors)]
    ring += [(2 * s + 1, (2 * s + 2) % (2 * sectors)) for s in range(sectors)]

    def arr(*shape, dtype=jnp.float32):
        return jax.ShapeDtypeStruct(shape, dtype)

    quarter = arr(5, half, axial, radial)
    ids = pltpu.VMEM((half, axial, radial), jnp.int32)
    keep, give = _call(
        pack_kernel, (quarter, quarter), 5, [ids, ids, pltpu.SemaphoreType.DMA((5, half, 2))],
        name="pack", space=pltpu.HBM,
    )(rhs_direct, rhs_adjoint, diag_shift, flame_gain, ref_owner)
    got = lax.ppermute(give, "flame", swap)
    edge = arr(5, half * HALO, width)
    first_rows, last_rows = _call(edges_kernel, (edge, edge), 2, name="edges")(keep, got)
    before = lax.ppermute(last_rows, "block", [(i, i + 1) for i in range(blocks - 1)])
    after = lax.ppermute(first_rows, "block", [(i + 1, i) for i in range(blocks - 1)])

    field, plane = arr(half, rows, width), arr(2, rows, width)
    full = pltpu.VMEM((half, rows, width), jnp.float32)
    message = arr(2 * blocks, 4, LANES)
    owners = arr(half, rows, width, dtype=jnp.int32)
    own_cells = pltpu.VMEM((half, axial, width), jnp.float32)
    hot = arr(half * axial, GROUP, width, dtype=jnp.bfloat16)
    high, low, sent = _call(
        hot_kernel, (hot, hot, message), 2,
        [pltpu.VMEM((1, axial, width), jnp.float32), own_cells, own_cells], name="hot",
    )(keep, got)
    bd, ba, gain, inverse, owner, direct, adjoint, inner, outer = _call(
        functools.partial(init_kernel, blocks=blocks),
        (field, field, field, field, owners, field, field, arr(5, INNER, rows, width), plane),
        4, [full, full], name="init",
    )(keep, got, before, after)
    sent, outer, inner = lax.optimization_barrier((sent, outer, inner))
    cut, layers = arr(2, half, axial, radial), (2, INNER, rows, width)
    everyone = 2 * blocks * sectors
    deep = halo = None
    for sweep in range(ITERS):
        outer_in = lax.ppermute(outer, ("sector", "flame"), ring)
        if sweep == 0:
            deep = lax.ppermute(inner, "flame", swap)
        elif sweep % INNER == 0:
            halo = lax.ppermute(halo, "flame", swap)
        recv = lax.all_to_all(sent, BF, 0, 0, tiled=True)
        args = (recv, outer_in, direct, adjoint, bd, ba, gain, inverse, owner, deep)
        args += () if halo is None else (halo,)
        if sweep < ITERS - 1:
            step = functools.partial(
                step_kernel, extra=INNER - 1 - sweep % INNER, first=sweep == 0
            )
            scratch = [pltpu.VMEM(layers, jnp.float32)] if sweep == 0 else []
            direct, adjoint, halo, outer, sent = _call(
                step, (field, field, arr(*layers), plane, message), len(args) + 2, scratch, name="step"
            )(*args, high, low)
        else:
            keep, give, sent = _call(
                last_kernel, (cut, cut, arr(everyone, LANES)), 11, [full, full], name="last"
            )(*args)

    got = lax.ppermute(give, "flame", swap)
    recv = lax.all_to_all(sent, ("sector",) + BF, 0, 0, tiled=True)
    out = arr(planes, axial, radial)
    cells = planes * axial * radial * everyone
    return tuple(
        _call(
            functools.partial(fields_kernel, cells=cells, group=2 * blocks), (out, out), 5, name="fields"
        )(recv, keep, got, flame_gain, ref_owner)
    )


def solution(mesh):
    spec = P("sector", "block", "flame")
    return jax.shard_map(
        on_device,
        mesh=mesh,
        in_specs=(spec,) * 5,
        out_specs=(spec, spec),
        check_vma=False,
    )
```

```python
import functools

import jax
import jax.numpy as jnp
from jax import lax
from jax.experimental import pallas as pl
from jax.experimental.pallas import tpu as pltpu
from jax.sharding import PartitionSpec as P

ITERS = 6
REF_DEV = 8
GROUP = 16
INNER = 3
PAD = 8
HALO = 6
LANES = 128
INTERPRET = False
BF = ("block", "flame")


def _call(kernel, out_shape, n_in, scratch=(), name=None, space=pltpu.VMEM):
    vmem = pl.BlockSpec(memory_space=pltpu.VMEM)
    single = not isinstance(out_shape, (tuple, list))

    def body(*refs):
        kernel([lax.axis_index(axis) for axis in ("flame", "block", "sector")], *refs)

    call = pl.pallas_call(
        body,
        out_shape=out_shape,
        in_specs=[pl.BlockSpec(memory_space=space)] * n_in,
        out_specs=vmem if single else [vmem] * len(out_shape),
        scratch_shapes=list(scratch),
        interpret=INTERPRET,
        name=name,
        compiler_params=pltpu.CompilerParams(vmem_limit_bytes=24 << 20),
    )
    if space is pltpu.VMEM or INTERPRET:
        return call
    return lambda *args: call(*(pltpu.with_memory_space_constraint(x, space) for x in args))


def _lookup(table, owner):
    low = jnp.take_along_axis(table[0], owner & (LANES - 1), axis=1, mode="promise_in_bounds")
    high = jnp.take_along_axis(table[1], owner & (LANES - 1), axis=1, mode="promise_in_bounds")
    return jnp.where(owner < LANES, low, high)


def _table(total, row):
    return [jnp.broadcast_to(total[row + j : row + j + 1], (8, LANES)) for j in (0, 1)]


def pack_kernel(here, *refs):
    core = here[0]
    ins, (keep_ref, give_ref, keep_id, give_id, sems) = refs[:5], refs[5:]
    half = keep_ref.shape[1]
    copies = []
    for i, ref in enumerate(ins):
        for p in range(half):
            step = 2 * half - 1 - 2 * p
            for k, (dst, ids, at) in enumerate(
                ((keep_ref, keep_id, core), (give_ref, give_id, 1 - core))
            ):
                to = dst.at[i, p] if i < 4 else ids.at[p]
                copies.append(pltpu.make_async_copy(ref.at[p + at * step], to, sems.at[i, p, k]))
    for copy in copies:
        copy.start()
    for copy in copies:
        copy.wait()
    keep_ref[4] = keep_id[...].astype(jnp.float32)
    give_ref[4] = give_id[...].astype(jnp.float32)


def _halo_rows(half):
    at = 0
    for i in range(5):
        depth = HALO if i < 3 else HALO - 1
        for p in range(half):
            yield i, p, depth, at
            at += depth


def edges_kernel(here, keep_ref, got_ref, after_ref, before_ref):
    core = here[0]
    _, half, axial, radial = keep_ref.shape
    for i, p, depth, at in _halo_rows(half):
        for ref, rng in ((after_ref, slice(0, depth)), (before_ref, slice(axial - depth, axial))):
            mine, other = keep_ref[i, p, rng], got_ref[i, p, rng]
            ref[at : at + depth, :radial] = jnp.where(core == 0, mine, other)
            ref[at : at + depth, radial:] = jnp.where(core == 0, other, mine)


def hot_kernel(here, keep_ref, got_ref, high_ref, low_ref, out_ref, d_ref, a_ref, gain_ref):
    core = here[0]
    count, half, axial, radial = keep_ref.shape
    width = 2 * radial
    ids = lax.broadcasted_iota(jnp.int32, (GROUP, width), 0).astype(jnp.float32)
    for p in range(half):
        for t in range(axial // 8):
            rng = slice(8 * t, 8 * t + 8)
            bd, ba, shift, gain, owner = (
                jnp.concatenate(
                    [jnp.where(core == h, keep_ref[i, p, rng], got_ref[i, p, rng]) for h in (0, 1)], axis=1
                )
                for i in range(count)
            )
            inv = 1.0 / (6.0 + shift)
            if p == 0:
                d_ref[0, rng] = bd * inv
            a_ref[p, rng] = ba * inv
            gain_ref[p, rng] = gain
            owner = owner.astype(jnp.int32)
            for part, ref in ((owner // GROUP, high_ref), (owner % GROUP, low_ref)):
                part = part.astype(jnp.float32)
                for x in range(8):
                    hit = jnp.broadcast_to(part[x : x + 1], (GROUP, width)) == ids
                    ref[(p * (axial // 8) + t) * 8 + x] = jnp.where(hit, 1.0, 0.0).astype(jnp.bfloat16)
    collect = _Collect(gain_ref, high_ref, low_ref, 0)
    for p in range(half):
        for t in range(axial // 8):
            collect.tile(p, t, a_ref[p, 8 * t : 8 * t + 8])
    collect.finish(out_ref)
    _write_refs(here, d_ref, out_ref, 0)


def init_kernel(here, keep_ref, got_ref, before_ref, after_ref, bd_ref, ba_ref, gain_ref,
                inv_ref, own_ref, d_ref, a_ref, inner_ref, outer_ref, shift_ref, id_ref, *, blocks):
    core, block = here[0], here[1]
    _, half, axial, radial = keep_ref.shape
    rows = axial + 2 * PAD
    arrays = (bd_ref, ba_ref, shift_ref, gain_ref, id_ref)
    for i, p, depth, at in _halo_rows(half):
        ref = arrays[i]
        ref[p, :PAD] = jnp.zeros((PAD, 2 * radial), jnp.float32)
        ref[p, rows - PAD :] = jnp.zeros((PAD, 2 * radial), jnp.float32)
        ref[p, PAD - depth : PAD] = before_ref[at : at + depth]
        ref[p, rows - PAD : rows - PAD + depth] = after_ref[at : at + depth]
        mine, other = keep_ref[i, p], got_ref[i, p]
        ref[p, PAD : PAD + axial, :radial] = jnp.where(core == 0, mine, other)
        ref[p, PAD : PAD + axial, radial:] = jnp.where(core == 0, other, mine)
    for p in range(half):
        for t in range(rows // 8):
            at = (p, slice(8 * t, 8 * t + 8))
            inv = 1.0 / (6.0 + shift_ref[at])
            if t < PAD // 8:
                inv = jnp.where(block == 0, 0.0, inv)
            if t >= (rows - PAD) // 8:
                inv = jnp.where(block == blocks - 1, 0.0, inv)
            inv_ref[at] = inv
            own_ref[at] = id_ref[at].astype(jnp.int32)
            d_ref[at] = bd_ref[at] * inv
            a_ref[at] = ba_ref[at] * inv
    for i, ref in enumerate((bd_ref, ba_ref, inv_ref, gain_ref, id_ref)):
        for depth in range(INNER if i < 3 else INNER - 1):
            inner_ref[_deep(i, depth)] = ref[half - 1 - depth]
    _send(outer_ref, d_ref, a_ref)


def _deep(i, depth):
    return INNER * i + depth if i < 3 else 3 * INNER + (INNER - 1) * (i - 3) + depth


def _send(outer_ref, d_ref, a_ref):
    outer_ref[0] = d_ref[0]
    outer_ref[1] = a_ref[0]


def step_kernel(here, *refs, extra, first):
    refs = list(refs)
    ins = [refs.pop(0) for _ in range(10)]
    halo_ref = None if first else refs.pop(0)
    high_ref, low_ref = refs.pop(0), refs.pop(0)
    dn_ref, an_ref, hn_ref, outer_ref, out_ref = [refs.pop(0) for _ in range(5)]
    if first:
        halo_ref = refs.pop(0)
        for i in (0, 1):
            for depth in range(INNER):
                halo_ref[i, depth] = ins[9][_deep(i, depth)] * ins[9][_deep(2, depth)]
    collect = _Collect(ins[6], high_ref, low_ref, PAD)
    _sweep(here, *ins, halo_ref, dn_ref, an_ref, hn_ref, extra, 0, collect)
    if not extra:
        for i, ref in enumerate((dn_ref, an_ref)):
            for depth in range(INNER):
                hn_ref[i, depth] = ref[ref.shape[0] - 1 - depth]
    _send(outer_ref, dn_ref, an_ref)
    collect.finish(out_ref)
    _write_refs(here, dn_ref, out_ref, PAD)


def _sweep(here, recv_ref, outer_ref, d_ref, a_ref, bd_ref, ba_ref, gain_ref,
           inv_ref, own_ref, deep_ref, halo_ref, dn_ref, an_ref, hn_ref, extra, pad=0, collect=None):
    core, block = here[0], here[1]
    planes, rows, width = d_ref.shape
    tiles = rows // 8
    total = jnp.sum(recv_ref[...], axis=0)
    table = _table(total, 0)
    sums = _table(total, 2)
    lane = lax.broadcasted_iota(jnp.int32, (8, LANES), 1)
    sub = lax.broadcasted_iota(jnp.int32, (8, LANES), 0)
    spot = (lane % 32 == 0) & (sub == 0) & (core == 0)
    first = lax.broadcasted_iota(jnp.int32, (8, width), 1) == 0
    last = lax.broadcasted_iota(jnp.int32, (8, width), 1) == width - 1

    def source(blk):
        tab = jnp.where(blk < 8, sums[0], sums[1])
        parts = []
        for j in range(width // LANES):
            at = jnp.bitwise_and(blk, 7) * 16 + 4 * j + lane // 32
            got = jnp.take_along_axis(tab, at & (LANES - 1), axis=1, mode="promise_in_bounds")
            parts.append(jnp.where(spot, got, 0.0))
        return jnp.concatenate(parts, axis=1)

    def plane(ref, field, p, rng):
        if p < 0:
            return outer_ref[field, rng]
        return ref[p, rng] if p < planes else halo_ref[field, p - planes, rng]

    def near(ref, field, p, t, below, mid, above):
        if t == 0:
            back = pltpu.roll(mid, 1, 0)
        else:
            back = plane(ref, field, p, slice(8 * t - 1, 8 * t + 7))
        if t == tiles - 1:
            front = pltpu.roll(mid, 7, 0)
        else:
            front = plane(ref, field, p, slice(8 * t + 1, 8 * t + 9))
        left = jnp.where(first, 0.0, pltpu.roll(mid, 1, 1))
        right = jnp.where(last, 0.0, pltpu.roll(mid, width - 1, 1))
        return (below + above) + (back + front) + (left + right)

    own_tiles = range(PAD // 8, tiles - PAD // 8)
    rest = [t for t in range(tiles) if t not in own_tiles] if pad == 0 else []
    for t in list(own_tiles) + rest:
        rng = slice(8 * t, 8 * t + 8)
        window = [[plane(r, i, p, rng) for p in (-1, 0)] for i, r in enumerate((d_ref, a_ref))]
        for p in range(planes + extra):
            if p < planes:
                to_d, to_a = dn_ref.at[p, rng], an_ref.at[p, rng]
                bd, ba, gain, inv, own = (r[p, rng] for r in (bd_ref, ba_ref, gain_ref, inv_ref, own_ref))
            else:
                to_d, to_a = hn_ref.at[0, p - planes, rng], hn_ref.at[1, p - planes, rng]
                bd, ba, inv, gain, own = (deep_ref[_deep(i, p - planes), rng] for i in range(5))
                own = own.astype(jnp.int32)
            for i, r in enumerate((d_ref, a_ref)):
                window[i] = window[i][-2:] + [plane(r, i, p + 1, rng)]
            looked = jnp.concatenate(
                [_lookup(table, own[:, LANES * j : LANES * (j + 1)]) for j in range(width // LANES)],
                axis=1,
            )
            to_d[...] = (bd + near(d_ref, 0, p, t, *window[0]) + gain * looked) * inv
            acc = ba + near(a_ref, 1, p, t, *window[1])
            if p == 0 and t == PAD // 8:
                acc = acc + source(block)
            if p == 0 and t == tiles - PAD // 8:
                acc = acc + source(block + 1)
            acc = acc * inv
            to_a[...] = acc
            if collect is not None:
                collect.some()
                if p < planes and t in own_tiles:
                    collect.tile(p, t - PAD // 8, acc)


def _ref_values(d_ref, pad=PAD):
    width = d_ref.shape[2]
    lane = lax.broadcasted_iota(jnp.int32, (8, LANES), 1)
    row = d_ref[0, pad : pad + 8]
    got = jnp.zeros((8, LANES), jnp.float32)
    for j in range(width // LANES):
        part = jnp.broadcast_to(row[0:1, LANES * j : LANES * (j + 1)], (8, LANES))
        pick = jnp.take_along_axis(part, (lane & 3) * 32, axis=1, mode="promise_in_bounds")
        got = jnp.where((lane & 15) // 4 == j, pick, got)
    return lane, got


def _write_refs(here, d_ref, out_ref, pad):
    core, block = here[0], here[1]
    lane, got = _ref_values(d_ref, pad)
    for half in (0, 1):
        mine = (lane // 16 + 8 * half == block) & (core == 0)
        out_ref[:, half] = jnp.broadcast_to(
            jnp.where(mine, got, 0.0)[0:1], (out_ref.shape[0], LANES)
        )


class _Collect:

    def __init__(self, gain_ref, high_ref, low_ref, pad):
        self.gain, self.hot, self.pad = gain_ref, (high_ref, low_ref), pad
        self.todo = []
        self.acc = jnp.zeros((2 * GROUP, GROUP), jnp.float32)

    def tile(self, p, t, a):
        gain_ref, tiles = self.gain, (self.gain.shape[1] - 2 * self.pad) // 8
        y = gain_ref[p, self.pad + 8 * t : self.pad + 8 * t + 8] * a
        coarse = y.astype(jnp.bfloat16).astype(jnp.float32)
        self.todo += [((p * tiles + t) * 8 + x, x, coarse, y - coarse) for x in range(8)]

    def some(self, count=4):
        now, self.todo = self.todo[:count], self.todo[count:]
        for line, x, coarse, fine in now:
            high = self.hot[0][line]
            vals = jnp.concatenate(
                [
                    high * jnp.broadcast_to(v[x : x + 1], high.shape).astype(jnp.bfloat16)
                    for v in (coarse, fine)
                ],
                axis=0,
            )
            self.acc = self.acc + lax.dot_general(
                vals, self.hot[1][line], (((1,), (1,)), ((), ())), preferred_element_type=jnp.float32
            )

    def finish(self, out_ref):
        self.some(len(self.todo))
        both = self.acc[:GROUP] + self.acc[GROUP:]
        both = jnp.concatenate([both, jnp.zeros((GROUP, LANES - GROUP), jnp.float32)], axis=1)
        sub = lax.broadcasted_iota(jnp.int32, (8, LANES), 0)
        for h in (0, 1):
            part = both[8 * h : 8 * h + 8]
            flat = part
            for i in range(1, 8):
                flat = jnp.where(sub == i, pltpu.roll(part, GROUP * i, 1), flat)
            out_ref[:, 2 + h] = jnp.broadcast_to(
                jnp.sum(flat, axis=0, keepdims=True), (out_ref.shape[0], LANES)
            )


def last_kernel(here, *refs):
    ins, (keep_ref, give_ref, out_ref, dn_ref, an_ref) = refs[:-5], refs[-5:]
    core, block = here[0], here[1]
    _sweep(here, *ins, dn_ref, an_ref, None, 0, PAD)
    planes, rows, width = dn_ref.shape
    radial = width // 2
    lane, values = _ref_values(dn_ref)
    line = jnp.where((lane // 16 == jnp.bitwise_and(block, 3)) & (core == 0), values, 0.0)[0:1]
    for i, ref in enumerate((dn_ref, an_ref)):
        acc = jnp.zeros((8, width), jnp.float32)
        for p in range(planes):
            for t in range((rows - 2 * PAD) // 8):
                v = ref[p, PAD + 8 * t : PAD + 8 * t + 8]
                acc = acc + v * v
                low, high = v[:, :radial], v[:, radial:]
                keep_ref[i, p, 8 * t : 8 * t + 8] = jnp.where(core == 0, low, high)
                give_ref[i, p, 8 * t : 8 * t + 8] = jnp.where(core == 0, high, low)
        acc = sum(acc[:, LANES * j : LANES * (j + 1)] for j in range(width // LANES))
        acc = acc + pltpu.roll(acc, 64, 1)
        acc = jnp.sum(acc + pltpu.roll(acc, 32, 1), axis=0, keepdims=True)
        line = jnp.where(lane[0:1] // 32 == 2 + i, acc, line)
    out_ref[...] = jnp.broadcast_to(line, out_ref.shape)


def fields_kernel(here, recv_ref, keep_ref, got_ref, gain_ref, own_ref, first_ref, second_ref,
                  *, cells, group):
    core, sector = here[0], here[2]
    planes, axial, radial = gain_ref.shape
    half = planes // 2
    lane = lax.broadcasted_iota(jnp.int32, (8, LANES), 1)
    quads = [
        jnp.broadcast_to(
            jnp.sum(recv_ref[pl.ds(pl.multiple_of(sector * group, 8) + 8 * j, 8), :], axis=0, keepdims=True),
            (8, LANES),
        )
        for j in range(4)
    ]
    table = [jnp.where(lane < 64, quads[2 * j], pltpu.roll(quads[2 * j + 1], 64, 1)) for j in (0, 1)]
    total = jnp.broadcast_to(jnp.sum(recv_ref[...], axis=0, keepdims=True), (8, LANES))
    squares = [
        jnp.sum(jnp.where(lane // 32 == 2 + i, total, 0.0), axis=1, keepdims=True)[0:1] / cells
        for i in (0, 1)
    ]
    scale = lax.rsqrt(squares[0] * squares[1] + 1e-12)
    for p in range(planes):
        for t in range(axial // 8):
            rng = slice(8 * t, 8 * t + 8)
            mine, at = (core == 0, p) if p < half else (core == 1, planes - 1 - p)
            direct, adjoint = (
                jnp.where(mine, keep_ref[i, at, rng], got_ref[i, at, rng]) for i in (0, 1)
            )
            own = own_ref[p, rng]
            looked = jnp.concatenate(
                [_lookup(table, own[:, LANES * j : LANES * (j + 1)]) for j in range(radial // LANES)],
                axis=1,
            )
            first_ref[p, rng] = adjoint * direct * scale
            second_ref[p, rng] = adjoint * (gain_ref[p, rng] * looked) * scale


def on_device(rhs_direct, rhs_adjoint, diag_shift, flame_gain, ref_owner):
    planes, axial, radial = rhs_direct.shape
    sectors, blocks = lax.axis_size("sector"), lax.axis_size("block")
    half, width, rows = planes // 2, 2 * radial, axial + 2 * PAD
    swap = [(0, 1), (1, 0)]
    ring = [(2 * s, (2 * s - 1) % (2 * sectors)) for s in range(sectors)]
    ring += [(2 * s + 1, (2 * s + 2) % (2 * sectors)) for s in range(sectors)]

    def arr(*shape, dtype=jnp.float32):
        return jax.ShapeDtypeStruct(shape, dtype)

    quarter = arr(5, half, axial, radial)
    ids = pltpu.VMEM((half, axial, radial), jnp.int32)
    keep, give = _call(
        pack_kernel, (quarter, quarter), 5, [ids, ids, pltpu.SemaphoreType.DMA((5, half, 2))],
        name="pack", space=pltpu.HBM,
    )(rhs_direct, rhs_adjoint, diag_shift, flame_gain, ref_owner)
    got = lax.ppermute(give, "flame", swap)
    edge = arr(half * (5 * HALO - 2), width)
    first_rows, last_rows = _call(edges_kernel, (edge, edge), 2, name="edges")(keep, got)
    before = lax.ppermute(last_rows, "block", [(i, i + 1) for i in range(blocks - 1)])
    after = lax.ppermute(first_rows, "block", [(i + 1, i) for i in range(blocks - 1)])

    field, plane = arr(half, rows, width), arr(2, rows, width)
    full = pltpu.VMEM((half, rows, width), jnp.float32)
    message = arr(2 * blocks, 4, LANES)
    owners = arr(half, rows, width, dtype=jnp.int32)
    own_cells = pltpu.VMEM((half, axial, width), jnp.float32)
    hot = arr(half * axial, GROUP, width, dtype=jnp.bfloat16)
    high, low, sent = _call(
        hot_kernel, (hot, hot, message), 2,
        [pltpu.VMEM((1, axial, width), jnp.float32), own_cells, own_cells], name="hot",
    )(keep, got)
    bd, ba, gain, inverse, owner, direct, adjoint, inner, outer = _call(
        functools.partial(init_kernel, blocks=blocks),
        (field, field, field, field, owners, field, field, arr(5 * INNER - 2, rows, width), plane),
        4, [full, full], name="init",
    )(keep, got, before, after)
    sent, outer, inner = lax.optimization_barrier((sent, outer, inner))
    cut, layers = arr(2, half, axial, radial), (2, INNER, rows, width)
    everyone = 2 * blocks * sectors
    deep = halo = None
    for sweep in range(ITERS):
        outer_in = lax.ppermute(outer, ("sector", "flame"), ring)
        if sweep == 0:
            deep = lax.ppermute(inner, "flame", swap)
        elif sweep % INNER == 0:
            halo = lax.ppermute(halo, "flame", swap)
        recv = lax.all_to_all(sent, BF, 0, 0, tiled=True)
        args = (recv, outer_in, direct, adjoint, bd, ba, gain, inverse, owner, deep)
        args += () if halo is None else (halo,)
        if sweep < ITERS - 1:
            step = functools.partial(
                step_kernel, extra=INNER - 1 - sweep % INNER, first=sweep == 0
            )
            scratch = [pltpu.VMEM(layers, jnp.float32)] if sweep == 0 else []
            direct, adjoint, halo, outer, sent = _call(
                step, (field, field, arr(*layers), plane, message), len(args) + 2, scratch, name="step"
            )(*args, high, low)
        else:
            keep, give, sent = _call(
                last_kernel, (cut, cut, arr(everyone, LANES)), 11, [full, full], name="last"
            )(*args)

    got = lax.ppermute(give, "flame", swap)
    recv = lax.all_to_all(sent, ("sector",) + BF, 0, 0, tiled=True)
    out = arr(planes, axial, radial)
    cells = planes * axial * radial * everyone
    return tuple(
        _call(
            functools.partial(fields_kernel, cells=cells, group=2 * blocks), (out, out), 5, name="fields"
        )(recv, keep, got, flame_gain, ref_owner)
    )


def solution(mesh):
    spec = P("sector", "block", "flame")
    return jax.shard_map(
        on_device,
        mesh=mesh,
        in_specs=(spec,) * 5,
        out_specs=(spec, spec),
        check_vma=False,
    )
```

```python
import functools

import jax
import jax.numpy as jnp
from jax import lax
from jax.experimental import pallas as pl
from jax.experimental.pallas import tpu as pltpu
from jax.sharding import PartitionSpec as P

ITERS = 6
REF_DEV = 8
GROUP = 16
INNER = 3
PAD = 8
HALO = 6
LANES = 128
INTERPRET = False
BF = ("block", "flame")


def _call(kernel, out_shape, n_in, scratch=(), name=None, space=pltpu.VMEM):
    vmem = pl.BlockSpec(memory_space=pltpu.VMEM)
    single = not isinstance(out_shape, (tuple, list))

    def body(*refs):
        kernel([lax.axis_index(axis) for axis in ("flame", "block", "sector")], *refs)

    call = pl.pallas_call(
        body,
        out_shape=out_shape,
        in_specs=[pl.BlockSpec(memory_space=space)] * n_in,
        out_specs=vmem if single else [vmem] * len(out_shape),
        scratch_shapes=list(scratch),
        interpret=INTERPRET,
        name=name,
        compiler_params=pltpu.CompilerParams(vmem_limit_bytes=24 << 20),
    )
    if space is pltpu.VMEM or INTERPRET:
        return call
    return lambda *args: call(*(pltpu.with_memory_space_constraint(x, space) for x in args))


def _lookup(table, owner):
    low = jnp.take_along_axis(table[0], owner & (LANES - 1), axis=1, mode="promise_in_bounds")
    high = jnp.take_along_axis(table[1], owner & (LANES - 1), axis=1, mode="promise_in_bounds")
    return jnp.where(owner < LANES, low, high)


def _table(total, row):
    return [jnp.broadcast_to(total[row + j : row + j + 1], (8, LANES)) for j in (0, 1)]


def pack_kernel(here, *refs):
    core = here[0]
    ins, (keep_ref, give_ref, keep_id, give_id, sems) = refs[:5], refs[5:]
    half = keep_ref.shape[1]
    copies = []
    for i, ref in enumerate(ins):
        for p in range(half):
            step = 2 * half - 1 - 2 * p
            for k, (dst, ids, at) in enumerate(
                ((keep_ref, keep_id, core), (give_ref, give_id, 1 - core))
            ):
                to = dst.at[i, p] if i < 4 else ids.at[p]
                copies.append(pltpu.make_async_copy(ref.at[p + at * step], to, sems.at[i, p, k]))
    for copy in copies:
        copy.start()
    for copy in copies:
        copy.wait()
    keep_ref[4] = keep_id[...].astype(jnp.float32)
    give_ref[4] = give_id[...].astype(jnp.float32)


def _halo_rows(half):
    at = 0
    for i in range(5):
        depth = HALO if i < 3 else HALO - 1
        for p in range(half):
            yield i, p, depth, at
            at += depth


def edges_kernel(here, keep_ref, got_ref, after_ref, before_ref):
    core = here[0]
    _, half, axial, radial = keep_ref.shape
    for i, p, depth, at in _halo_rows(half):
        for ref, rng in ((after_ref, slice(0, depth)), (before_ref, slice(axial - depth, axial))):
            mine, other = keep_ref[i, p, rng], got_ref[i, p, rng]
            ref[at : at + depth, :radial] = jnp.where(core == 0, mine, other)
            ref[at : at + depth, radial:] = jnp.where(core == 0, other, mine)


def hot_kernel(here, keep_ref, got_ref, high_ref, low_ref, out_ref, d_ref, a_ref, gain_ref):
    core = here[0]
    count, half, axial, radial = keep_ref.shape
    width = 2 * radial
    ids = lax.broadcasted_iota(jnp.int32, (GROUP, width), 0).astype(jnp.float32)
    for p in range(half):
        for t in range(axial // 8):
            rng = slice(8 * t, 8 * t + 8)
            bd, ba, shift, gain, owner = (
                jnp.concatenate(
                    [jnp.where(core == h, keep_ref[i, p, rng], got_ref[i, p, rng]) for h in (0, 1)], axis=1
                )
                for i in range(count)
            )
            inv = 1.0 / (6.0 + shift)
            if p == 0:
                d_ref[0, rng] = bd * inv
            a_ref[p, rng] = ba * inv
            gain_ref[p, rng] = gain
            owner = owner.astype(jnp.int32)
            for part, ref in ((owner // GROUP, high_ref), (owner % GROUP, low_ref)):
                part = part.astype(jnp.float32)
                for x in range(8):
                    hit = jnp.broadcast_to(part[x : x + 1], (GROUP, width)) == ids
                    ref[(p * (axial // 8) + t) * 8 + x] = jnp.where(hit, 1.0, 0.0).astype(jnp.bfloat16)
    collect = _Collect(gain_ref, high_ref, low_ref, 0)
    for p in range(half):
        for t in range(axial // 8):
            collect.tile(p, t, a_ref[p, 8 * t : 8 * t + 8])
    collect.finish(out_ref)
    _write_refs(here, d_ref, out_ref, 0)


def init_kernel(here, keep_ref, got_ref, before_ref, after_ref, bd_ref, ba_ref, gain_ref,
                inv_ref, own_ref, d_ref, a_ref, inner_ref, outer_ref, shift_ref, id_ref, *, blocks):
    core, block = here[0], here[1]
    _, half, axial, radial = keep_ref.shape
    rows = axial + 2 * PAD
    arrays = (bd_ref, ba_ref, shift_ref, gain_ref, id_ref)
    for i, p, depth, at in _halo_rows(half):
        ref = arrays[i]
        ref[p, :PAD] = jnp.zeros((PAD, 2 * radial), jnp.float32)
        ref[p, rows - PAD :] = jnp.zeros((PAD, 2 * radial), jnp.float32)
        ref[p, PAD - depth : PAD] = before_ref[at : at + depth]
        ref[p, rows - PAD : rows - PAD + depth] = after_ref[at : at + depth]
        mine, other = keep_ref[i, p], got_ref[i, p]
        ref[p, PAD : PAD + axial, :radial] = jnp.where(core == 0, mine, other)
        ref[p, PAD : PAD + axial, radial:] = jnp.where(core == 0, other, mine)
    for p in range(half):
        for t in range(rows // 8):
            at = (p, slice(8 * t, 8 * t + 8))
            inv = 1.0 / (6.0 + shift_ref[at])
            if t < PAD // 8:
                inv = jnp.where(block == 0, 0.0, inv)
            if t >= (rows - PAD) // 8:
                inv = jnp.where(block == blocks - 1, 0.0, inv)
            inv_ref[at] = inv
            own_ref[at] = id_ref[at].astype(jnp.int32)
            d_ref[at] = bd_ref[at] * inv
            a_ref[at] = ba_ref[at] * inv
    for i, ref in enumerate((bd_ref, ba_ref, inv_ref, gain_ref, id_ref)):
        for depth in range(INNER if i < 3 else INNER - 1):
            inner_ref[_deep(i, depth)] = ref[half - 1 - depth]
    _send(outer_ref, d_ref, a_ref)


def _deep(i, depth):
    return INNER * i + depth if i < 3 else 3 * INNER + (INNER - 1) * (i - 3) + depth


def _send(outer_ref, d_ref, a_ref):
    outer_ref[0] = d_ref[0]
    outer_ref[1] = a_ref[0]


def step_kernel(here, *refs, extra, first):
    refs = list(refs)
    ins = [refs.pop(0) for _ in range(10)]
    halo_ref = None if first else refs.pop(0)
    high_ref, low_ref = refs.pop(0), refs.pop(0)
    dn_ref, an_ref, hn_ref, outer_ref, out_ref = [refs.pop(0) for _ in range(5)]
    if first:
        halo_ref = refs.pop(0)
        for i in (0, 1):
            for depth in range(INNER):
                halo_ref[i, depth] = ins[9][_deep(i, depth)] * ins[9][_deep(2, depth)]
    collect = _Collect(ins[6], high_ref, low_ref, PAD)
    _sweep(here, *ins, halo_ref, dn_ref, an_ref, hn_ref, extra, 0, collect)
    if not extra:
        for i, ref in enumerate((dn_ref, an_ref)):
            for depth in range(INNER):
                hn_ref[i, depth] = ref[ref.shape[0] - 1 - depth]
    _send(outer_ref, dn_ref, an_ref)
    collect.finish(out_ref)
    _write_refs(here, dn_ref, out_ref, PAD)


def _sweep(here, recv_ref, outer_ref, d_ref, a_ref, bd_ref, ba_ref, gain_ref,
           inv_ref, own_ref, deep_ref, halo_ref, dn_ref, an_ref, hn_ref, extra, pad=0, collect=None):
    core, block = here[0], here[1]
    planes, rows, width = d_ref.shape
    tiles = rows // 8
    total = jnp.sum(recv_ref[...], axis=0)
    table = _table(total, 0)
    sums = _table(total, 2)
    lane = lax.broadcasted_iota(jnp.int32, (8, LANES), 1)
    sub = lax.broadcasted_iota(jnp.int32, (8, LANES), 0)
    spot = (lane % 32 == 0) & (sub == 0) & (core == 0)
    first = lax.broadcasted_iota(jnp.int32, (8, width), 1) == 0
    last = lax.broadcasted_iota(jnp.int32, (8, width), 1) == width - 1

    def source(blk):
        tab = jnp.where(blk < 8, sums[0], sums[1])
        parts = []
        for j in range(width // LANES):
            at = jnp.bitwise_and(blk, 7) * 16 + 4 * j + lane // 32
            got = jnp.take_along_axis(tab, at & (LANES - 1), axis=1, mode="promise_in_bounds")
            parts.append(jnp.where(spot, got, 0.0))
        return jnp.concatenate(parts, axis=1)

    def plane(ref, field, p, rng):
        if p < 0:
            return outer_ref[field, rng]
        return ref[p, rng] if p < planes else halo_ref[field, p - planes, rng]

    def near(ref, field, p, t, below, mid, above):
        if t == 0:
            back = pltpu.roll(mid, 1, 0)
        else:
            back = plane(ref, field, p, slice(8 * t - 1, 8 * t + 7))
        if t == tiles - 1:
            front = pltpu.roll(mid, 7, 0)
        else:
            front = plane(ref, field, p, slice(8 * t + 1, 8 * t + 9))
        left = jnp.where(first, 0.0, pltpu.roll(mid, 1, 1))
        right = jnp.where(last, 0.0, pltpu.roll(mid, width - 1, 1))
        return (below + above) + (back + front) + (left + right)

    own_tiles = range(PAD // 8, tiles - PAD // 8)
    rest = [t for t in range(tiles) if t not in own_tiles] if pad == 0 else []
    for t in list(own_tiles) + rest:
        rng = slice(8 * t, 8 * t + 8)
        window = [[plane(r, i, p, rng) for p in (-1, 0)] for i, r in enumerate((d_ref, a_ref))]
        for p in range(planes + extra):
            if p < planes:
                to_d, to_a = dn_ref.at[p, rng], an_ref.at[p, rng]
                bd, ba, gain, inv, own = (r[p, rng] for r in (bd_ref, ba_ref, gain_ref, inv_ref, own_ref))
            else:
                to_d, to_a = hn_ref.at[0, p - planes, rng], hn_ref.at[1, p - planes, rng]
                bd, ba, inv, gain, own = (deep_ref[_deep(i, p - planes), rng] for i in range(5))
                own = own.astype(jnp.int32)
            for i, r in enumerate((d_ref, a_ref)):
                window[i] = window[i][-2:] + [plane(r, i, p + 1, rng)]
            looked = jnp.concatenate(
                [_lookup(table, own[:, LANES * j : LANES * (j + 1)]) for j in range(width // LANES)],
                axis=1,
            )
            to_d[...] = (bd + near(d_ref, 0, p, t, *window[0]) + gain * looked) * inv
            acc = ba + near(a_ref, 1, p, t, *window[1])
            if p == 0 and t == PAD // 8:
                acc = acc + source(block)
            if p == 0 and t == tiles - PAD // 8:
                acc = acc + source(block + 1)
            acc = acc * inv
            to_a[...] = acc
            if collect is not None:
                collect.some()
                if p < planes and t in own_tiles:
                    collect.tile(p, t - PAD // 8, acc)


def _ref_values(d_ref, pad=PAD):
    width = d_ref.shape[2]
    lane = lax.broadcasted_iota(jnp.int32, (8, LANES), 1)
    row = d_ref[0, pad : pad + 8]
    got = jnp.zeros((8, LANES), jnp.float32)
    for j in range(width // LANES):
        part = jnp.broadcast_to(row[0:1, LANES * j : LANES * (j + 1)], (8, LANES))
        pick = jnp.take_along_axis(part, (lane & 3) * 32, axis=1, mode="promise_in_bounds")
        got = jnp.where((lane & 15) // 4 == j, pick, got)
    return lane, got


def _write_refs(here, d_ref, out_ref, pad):
    core, block = here[0], here[1]
    lane, got = _ref_values(d_ref, pad)
    for half in (0, 1):
        mine = (lane // 16 + 8 * half == block) & (core == 0)
        out_ref[:, half] = jnp.broadcast_to(
            jnp.where(mine, got, 0.0)[0:1], (out_ref.shape[0], LANES)
        )


class _Collect:

    def __init__(self, gain_ref, high_ref, low_ref, pad):
        self.gain, self.hot, self.pad = gain_ref, (high_ref, low_ref), pad
        self.todo = []
        self.acc = jnp.zeros((2 * GROUP, GROUP), jnp.float32)

    def tile(self, p, t, a):
        gain_ref, tiles = self.gain, (self.gain.shape[1] - 2 * self.pad) // 8
        y = gain_ref[p, self.pad + 8 * t : self.pad + 8 * t + 8] * a
        coarse = y.astype(jnp.bfloat16).astype(jnp.float32)
        self.todo += [((p * tiles + t) * 8 + x, x, coarse, y - coarse) for x in range(8)]

    def some(self, count=4):
        now, self.todo = self.todo[:count], self.todo[count:]
        for line, x, coarse, fine in now:
            high = self.hot[0][line]
            vals = jnp.concatenate(
                [
                    high * jnp.broadcast_to(v[x : x + 1], high.shape).astype(jnp.bfloat16)
                    for v in (coarse, fine)
                ],
                axis=0,
            )
            self.acc = self.acc + lax.dot_general(
                vals, self.hot[1][line], (((1,), (1,)), ((), ())), preferred_element_type=jnp.float32
            )

    def finish(self, out_ref):
        self.some(len(self.todo))
        both = self.acc[:GROUP] + self.acc[GROUP:]
        both = jnp.concatenate([both, jnp.zeros((GROUP, LANES - GROUP), jnp.float32)], axis=1)
        sub = lax.broadcasted_iota(jnp.int32, (8, LANES), 0)
        for h in (0, 1):
            part = both[8 * h : 8 * h + 8]
            flat = part
            for i in range(1, 8):
                flat = jnp.where(sub == i, pltpu.roll(part, GROUP * i, 1), flat)
            out_ref[:, 2 + h] = jnp.broadcast_to(
                jnp.sum(flat, axis=0, keepdims=True), (out_ref.shape[0], LANES)
            )


def last_kernel(here, *refs):
    ins, (keep_ref, give_ref, out_ref, dn_ref, an_ref) = refs[:-5], refs[-5:]
    core, block = here[0], here[1]
    _sweep(here, *ins, dn_ref, an_ref, None, 0, PAD)
    planes, rows, width = dn_ref.shape
    radial = width // 2
    lane, values = _ref_values(dn_ref)
    line = jnp.where((lane // 16 == jnp.bitwise_and(block, 3)) & (core == 0), values, 0.0)[0:1]
    for i, ref in enumerate((dn_ref, an_ref)):
        acc = jnp.zeros((8, width), jnp.float32)
        for p in range(planes):
            for t in range((rows - 2 * PAD) // 8):
                v = ref[p, PAD + 8 * t : PAD + 8 * t + 8]
                acc = acc + v * v
                low, high = v[:, :radial], v[:, radial:]
                keep_ref[i, p, 8 * t : 8 * t + 8] = jnp.where(core == 0, low, high)
                give_ref[i, p, 8 * t : 8 * t + 8] = jnp.where(core == 0, high, low)
        acc = sum(acc[:, LANES * j : LANES * (j + 1)] for j in range(width // LANES))
        acc = acc + pltpu.roll(acc, 64, 1)
        acc = jnp.sum(acc + pltpu.roll(acc, 32, 1), axis=0, keepdims=True)
        line = jnp.where(lane[0:1] // 32 == 2 + i, acc, line)
    out_ref[...] = jnp.broadcast_to(line, out_ref.shape)


def fields_kernel(here, recv_ref, keep_ref, got_ref, gain_ref, own_ref, first_ref, second_ref,
                  *, cells, group):
    core, sector = here[0], here[2]
    planes, axial, radial = gain_ref.shape
    half = planes // 2
    lane = lax.broadcasted_iota(jnp.int32, (8, LANES), 1)
    quads = [
        jnp.broadcast_to(
            jnp.sum(recv_ref[pl.ds(pl.multiple_of(sector * group, 8) + 8 * j, 8), :], axis=0, keepdims=True),
            (8, LANES),
        )
        for j in range(4)
    ]
    table = [jnp.where(lane < 64, quads[2 * j], pltpu.roll(quads[2 * j + 1], 64, 1)) for j in (0, 1)]
    total = jnp.broadcast_to(jnp.sum(recv_ref[...], axis=0, keepdims=True), (8, LANES))
    squares = [
        jnp.sum(jnp.where(lane // 32 == 2 + i, total, 0.0), axis=1, keepdims=True)[0:1] / cells
        for i in (0, 1)
    ]
    scale = lax.rsqrt(squares[0] * squares[1] + 1e-12)
    for p in range(planes):
        for t in range(axial // 8):
            rng = slice(8 * t, 8 * t + 8)
            mine, at = (core == 0, p) if p < half else (core == 1, planes - 1 - p)
            direct, adjoint = (
                jnp.where(mine, keep_ref[i, at, rng], got_ref[i, at, rng]) for i in (0, 1)
            )
            own = own_ref[p, rng]
            looked = jnp.concatenate(
                [_lookup(table, own[:, LANES * j : LANES * (j + 1)]) for j in range(radial // LANES)],
                axis=1,
            )
            first_ref[p, rng] = adjoint * direct * scale
            second_ref[p, rng] = adjoint * (gain_ref[p, rng] * looked) * scale


def on_device(rhs_direct, rhs_adjoint, diag_shift, flame_gain, ref_owner):
    planes, axial, radial = rhs_direct.shape
    sectors, blocks = lax.axis_size("sector"), lax.axis_size("block")
    half, width, rows = planes // 2, 2 * radial, axial + 2 * PAD
    swap = [(0, 1), (1, 0)]
    ring = [(2 * s, (2 * s - 1) % (2 * sectors)) for s in range(sectors)]
    ring += [(2 * s + 1, (2 * s + 2) % (2 * sectors)) for s in range(sectors)]

    def arr(*shape, dtype=jnp.float32):
        return jax.ShapeDtypeStruct(shape, dtype)

    quarter = arr(5, half, axial, radial)
    ids = pltpu.VMEM((half, axial, radial), jnp.int32)
    keep, give = _call(
        pack_kernel, (quarter, quarter), 5, [ids, ids, pltpu.SemaphoreType.DMA((5, half, 2))],
        name="pack", space=pltpu.HBM,
    )(rhs_direct, rhs_adjoint, diag_shift, flame_gain, ref_owner)
    got = lax.ppermute(give, "flame", swap)
    edge = arr(half * (5 * HALO - 2), width)
    first_rows, last_rows = _call(edges_kernel, (edge, edge), 2, name="edges")(keep, got)
    before = lax.ppermute(last_rows, "block", [(i, i + 1) for i in range(blocks - 1)])
    after = lax.ppermute(first_rows, "block", [(i + 1, i) for i in range(blocks - 1)])

    field, plane = arr(half, rows, width), arr(2, rows, width)
    full = pltpu.VMEM((half, rows, width), jnp.float32)
    message = arr(2 * blocks, 4, LANES)
    owners = arr(half, rows, width, dtype=jnp.int32)
    own_cells = pltpu.VMEM((half, axial, width), jnp.float32)
    hot = arr(half * axial, GROUP, width, dtype=jnp.bfloat16)
    high, low, sent = _call(
        hot_kernel, (hot, hot, message), 2,
        [pltpu.VMEM((1, axial, width), jnp.float32), own_cells, own_cells], name="hot",
    )(keep, got)
    bd, ba, gain, inverse, owner, direct, adjoint, inner, outer = _call(
        functools.partial(init_kernel, blocks=blocks),
        (field, field, field, field, owners, field, field, arr(5 * INNER - 2, rows, width), plane),
        4, [full, full], name="init",
    )(keep, got, before, after)
    cut, layers = arr(2, half, axial, radial), (2, INNER, rows, width)
    everyone = 2 * blocks * sectors
    deep = halo = None
    for sweep in range(ITERS):
        outer_in = lax.ppermute(outer, ("sector", "flame"), ring)
        if sweep == 0:
            deep = lax.ppermute(inner, "flame", swap)
        elif sweep % INNER == 0:
            halo = lax.ppermute(halo, "flame", swap)
        recv = lax.all_to_all(sent, BF, 0, 0, tiled=True)
        args = (recv, outer_in, direct, adjoint, bd, ba, gain, inverse, owner, deep)
        args += () if halo is None else (halo,)
        if sweep < ITERS - 1:
            step = functools.partial(
                step_kernel, extra=INNER - 1 - sweep % INNER, first=sweep == 0
            )
            scratch = [pltpu.VMEM(layers, jnp.float32)] if sweep == 0 else []
            direct, adjoint, halo, outer, sent = _call(
                step, (field, field, arr(*layers), plane, message), len(args) + 2, scratch, name="step"
            )(*args, high, low)
        else:
            keep, give, sent = _call(
                last_kernel, (cut, cut, arr(everyone, LANES)), 11, [full, full], name="last"
            )(*args)

    got = lax.ppermute(give, "flame", swap)
    recv = lax.all_to_all(sent, ("sector",) + BF, 0, 0, tiled=True)
    out = arr(planes, axial, radial)
    cells = planes * axial * radial * everyone
    return tuple(
        _call(
            functools.partial(fields_kernel, cells=cells, group=2 * blocks), (out, out), 5, name="fields"
        )(recv, keep, got, flame_gain, ref_owner)
    )


def solution(mesh):
    spec = P("sector", "block", "flame")
    return jax.shard_map(
        on_device,
        mesh=mesh,
        in_specs=(spec,) * 5,
        out_specs=(spec, spec),
        check_vma=False,
    )
```
